32 devices in a mesh: groups: 2 (over y), blk: 8 (over z, x), rep: 2 (over core).
Axes of the slice: x: 2, y: 2, z: 4, core: 2. Of those that a mesh axis runs over, the one named last changes fastest.
Arguments:
- tokens: bfloat16 [16384, 1024], P(('groups', 'blk', 'rep')), parts along dimension 0, may hold values from -6 to 6
- hidden_grad: bfloat16 [16384, 4096], P(('groups', 'blk', 'rep')), parts along dimension 0, may hold values from -6 to 6
- weights: bfloat16 [2, 4096, 1024], P(None, 'blk', 'rep'), may hold values from -0.1875 to 0.1875
- first_moment: float32 [2, 8192, 1024], P(None, ('groups', 'blk'), 'rep'), parts along dimension 1, may hold values from -0.0014648438 to 0.0014648438
- second_moment: float32 [2, 8192, 1024], P(None, ('groups', 'blk'), 'rep'), parts along dimension 1, may hold values from 1e-09 to 1e-07
Outputs:
- hidden: bfloat16 [16384, 4096], P(('groups', 'blk', 'rep')), parts along dimension 0
- adam_step: float32 [2, 8192, 1024], P(None, ('groups', 'blk')), parts along dimension 1
The draws below stay inside these ranges and needn't reach their ends.
There are 2 independent parts, one for each index of `groups`. The reference program is written for one: setup_inputs(seed, part) draws one part's arguments, and reference() takes and returns one part's arrays. A program takes and returns all parts, laid end to end along the dimension named above; an argument that names none is the same for every part. Nothing has to cross between parts.
All inputs are finite; a program needn't handle non-finite values.
Results may differ from the reference program's by a relative error of at most 0.0034.
Values may be sent and summed in bfloat16 or wider, within the bound.
A program may use at most 128 MiB of HBM per device.

```python
import math
import jax
import jax.numpy as jnp
from jax import lax

D = 1024
FW = 4096
TOK_DEV = 512
PANEL = 512
WINDOW = 8
TOKENS = 8192
N_BLK = 8
N_REP = 2


def levels(stream_key, shape, shards, least, top_value):
    loudness, own = 1.0, jax.random.fold_in(stream_key, 6)
    for position, parts in shards:
        steps = jnp.exp(jax.random.uniform(jax.random.fold_in(own, position), (parts,), jnp.float32, least / len(shards), top_value / len(shards)))
        loudness = loudness * jnp.repeat(steps, shape[position] // parts).reshape([-1 if axis == position else 1 for axis in range(len(shape))])
    return loudness


def gaussian(rng, shape, scale, bound, cuts=(), held_as=jnp.bfloat16):
    loudness = levels(rng, shape, cuts, -0.22, 0.18) if cuts else 1.0
    result = jax.random.normal(rng, shape, jnp.float32) * scale * loudness
    return jnp.minimum(jnp.maximum(result, -bound), bound).astype(held_as)


def setup_inputs(seed: int = 0, part: int = 0) -> dict:
    keys = jax.random.split(jax.random.key(seed), 6)
    part_splits = jax.random.split(jax.random.fold_in(keys[5], part), 6)
    tokens = gaussian(part_splits[0], (TOKENS, D), 1.0, 6.0, ((0, 16),))
    hidden_grad = gaussian(part_splits[1], (TOKENS, WINDOW * PANEL), 1.0, 6.0, ((0, 16),))
    weights = gaussian(keys[2], (2, FW, D), D ** -0.5, 0.1875, ((1, 8), (2, 2)))
    first_moment = gaussian(part_splits[3], (2, FW, D), 0.0001, 0.0014648438, ((1, 8), (2, 2)), jnp.float32)
    second_moment = jnp.clip(jnp.exp(math.log(1.0000000116860974e-07) - 4.6051702 * jax.random.uniform(part_splits[4], (2, FW, D), jnp.float32) ** levels(part_splits[4], (2, FW, D), ((1, 8), (2, 2)), -0.2, 0.2)), 9.999999717180685e-10, 1.0000000116860974e-07)
    return {"tokens": tokens, "hidden_grad": hidden_grad, "weights": weights, "first_moment": first_moment, "second_moment": second_moment}


clip_norm = 1.0
beta_one = 0.9
beta_two = 0.95
step_count = 10.0
adam_eps = 1e-08
decay_rate = 0.1

def swiglu_terms(tokens, incoming_grad, gate_rows, up_rows):
    contract = (((1,), (1,)), ((), ()))
    gate = lax.dot_general(tokens, gate_rows, contract, preferred_element_type=jnp.float32)
    upper = lax.dot_general(tokens, up_rows, contract, preferred_element_type=jnp.float32)
    sigma = jax.nn.sigmoid(gate)
    activated = gate * sigma
    hidden = (activated * upper).astype(jnp.bfloat16)
    incoming = incoming_grad.astype(jnp.float32)
    gate_grad = (incoming * upper * sigma * (1.0 + gate * (1.0 - sigma))).astype(jnp.bfloat16)
    up_grad = (incoming * activated).astype(jnp.bfloat16)
    return (hidden, gate_grad, up_grad)

def adam_update(gradient, first_moment, second_moment, weights, norm_sq):
    clip_scale = jnp.minimum(1.0, clip_norm / jnp.sqrt(norm_sq))
    clipped = gradient * clip_scale
    first = beta_one * first_moment + (1.0 - beta_one) * clipped
    second = beta_two * second_moment + (1.0 - beta_two) * clipped * clipped
    first_hat = first / (1.0 - beta_one ** step_count)
    second_hat = second / (1.0 - beta_two ** step_count)
    return first_hat / (jnp.sqrt(second_hat) + adam_eps) + decay_rate * weights.astype(jnp.float32)

def reference(tokens, hidden_grad, weights, first_moment, second_moment):
    block_rows = N_REP * TOK_DEV
    token_blocks = tokens.reshape(N_BLK, block_rows, D)
    grad_blocks = hidden_grad.reshape(N_BLK, block_rows, WINDOW, PANEL)
    panels = weights.reshape(2, N_BLK, PANEL, D)
    contract = (((0,), (0,)), ((), ()))

    def visit(gradient, inputs):
        block_index, block_tokens, block_grad = inputs
        slot_outs = []
        for slot in range(WINDOW):
            owner = jnp.mod(block_index - slot, N_BLK).astype(jnp.int32)
            panel_rows = lax.dynamic_index_in_dim(panels, owner, 1, keepdims=False)
            hidden, gate_grad, up_grad = swiglu_terms(block_tokens, block_grad[:, slot, :], panel_rows[0], panel_rows[1])
            gate_term = lax.dot_general(gate_grad, block_tokens, contract, preferred_element_type=jnp.float32)
            up_term = lax.dot_general(up_grad, block_tokens, contract, preferred_element_type=jnp.float32)
            current = lax.dynamic_index_in_dim(gradient, owner, 1, keepdims=False)
            updated = current + jnp.stack([gate_term, up_term], axis=0)
            gradient = lax.dynamic_update_index_in_dim(gradient, updated, owner, 1)
            slot_outs.append(hidden)
        return (gradient, jnp.stack(slot_outs, axis=1))
    initial = jnp.zeros((2, N_BLK, PANEL, D), jnp.float32)
    block_ids = jnp.arange(N_BLK, dtype=jnp.int32)
    gradient, hidden = lax.scan(visit, initial, (block_ids, token_blocks, grad_blocks))
    hidden = hidden.reshape(TOKENS, WINDOW * PANEL)
    gradient = gradient.reshape(2, FW, D)
    norm_sq = jnp.sum(gradient * gradient)
    adam_step = adam_update(gradient, first_moment, second_moment, weights, norm_sq)
    return (hidden, adam_step)
```

```python
import jax
import jax.numpy as jnp
from jax import lax
from jax.sharding import PartitionSpec as P

clip_norm = 1.0
beta_one = 0.9
beta_two = 0.95
step_count = 10.0
adam_eps = 1e-08
decay_rate = 0.1


def shifted(value, axis, by):
    devices = lax.axis_size(axis)
    return lax.ppermute(value, axis, [(i, (i + by) % devices) for i in range(devices)])


def swiglu_terms(tokens, incoming_grad, gate_rows, up_rows):
    contract = (((1,), (1,)), ((), ()))
    gate = lax.dot_general(tokens, gate_rows, contract, preferred_element_type=jnp.float32)
    upper = lax.dot_general(tokens, up_rows, contract, preferred_element_type=jnp.float32)
    sigma = jax.nn.sigmoid(gate)
    activated = gate * sigma
    hidden = (activated * upper).astype(jnp.bfloat16)
    incoming = incoming_grad.astype(jnp.float32)
    gate_grad = (incoming * upper * sigma * (1.0 + gate * (1.0 - sigma))).astype(jnp.bfloat16)
    up_grad = (incoming * activated).astype(jnp.bfloat16)
    return (hidden, gate_grad, up_grad)


def adam_update(gradient, first_moment, second_moment, weights, norm_sq):
    clip_scale = jnp.minimum(1.0, clip_norm / jnp.sqrt(norm_sq))
    clipped = gradient * clip_scale
    first = beta_one * first_moment + (1.0 - beta_one) * clipped
    second = beta_two * second_moment + (1.0 - beta_two) * clipped * clipped
    first_hat = first / (1.0 - beta_one**step_count)
    second_hat = second / (1.0 - beta_two**step_count)
    return first_hat / (jnp.sqrt(second_hat) + adam_eps) + decay_rate * weights.astype(jnp.float32)


def on_device(tokens, hidden_grad, weights, first_moment, second_moment):
    unit_count = weights.shape[1]
    token_count = tokens.shape[0]
    slot_count = hidden_grad.shape[1] // unit_count
    own_full = lax.all_gather(weights, "rep", axis=2, tiled=True)
    slot_grads = jnp.swapaxes(hidden_grad.reshape(token_count, slot_count, unit_count), 0, 1)
    contract = (((1,), (0,)), ((), ()))

    def grad_term(gate_grad, up_grad):
        paired = jnp.stack([gate_grad, up_grad], axis=0)
        return lax.dot_general(paired, tokens, contract, preferred_element_type=jnp.float32)

    zero_sums = jnp.zeros((2, unit_count, tokens.shape[1]), jnp.float32)

    def visit(panel_rows, slot_grad):
        hidden, gate_grad, up_grad = swiglu_terms(tokens, slot_grad, panel_rows[0], panel_rows[1])
        arrived = shifted(panel_rows, "blk", 1)
        return (arrived, (hidden, gate_grad, up_grad))

    _, (hidden_slots, gate_slots, up_slots) = lax.scan(visit, own_full, slot_grads)

    def collect(running, grads_pair):
        arrived = shifted(running, "blk", -1)
        return (arrived + grad_term(grads_pair[0], grads_pair[1]), None)

    owned_sums, _ = lax.scan(collect, zero_sums, (gate_slots, up_slots), reverse=True)
    hidden = jnp.swapaxes(hidden_slots, 0, 1).reshape(token_count, slot_count * unit_count)
    gradient = lax.psum_scatter(owned_sums, "rep", scatter_dimension=2, tiled=True)
    norm_sq = lax.psum(jnp.sum(gradient * gradient), ("blk", "rep"))
    update = adam_update(gradient, first_moment, second_moment, weights, norm_sq)
    adam_step = lax.all_gather(update, "rep", axis=2, tiled=True)
    return (hidden, adam_step)


def ring_order(devices):
    return list(range(0, devices, 2)) + list(range(devices - 1, 0, -2))


def on_ring(tokens, hidden_grad, weights, first_moment, second_moment):
    devices = lax.axis_size("blk")
    half = devices // 2
    units, features = weights.shape[1], weights.shape[2]
    order = ring_order(devices)
    blk, rep = lax.axis_index("blk"), lax.axis_index("rep")
    positions = [order.index(i) for i in range(devices)]
    pos = jnp.array(positions, jnp.int32)[blk]

    def hop(value, by):
        return lax.ppermute(value, "blk", [(order[i], order[(i + by) % devices]) for i in range(devices)])

    def partner(value):
        return lax.ppermute(value, "rep", [(0, 1), (1, 0)])

    def joined(mine, other):
        first = rep == 0
        return jnp.concatenate([jnp.where(first, mine, other), jnp.where(first, other, mine)], axis=-1)

    own_tokens = lax.dynamic_slice_in_dim(tokens, rep * features, features, 1)
    other_tokens = lax.dynamic_slice_in_dim(tokens, (1 - rep) * features, features, 1)

    panels = {0: weights}
    for k in range(1, half):
        panels[k] = hop(panels[k - 1], 1)
        panels[-k] = hop(panels[1 - k], -1)
    panels[half] = (hop(panels[half - 1][0], 1), hop(panels[1 - half][1], -1))

    def rows(own, other):
        contract = (((1,), (1,)), ((), ()))
        return lax.dot_general(own_tokens, own, contract, preferred_element_type=jnp.float32) + lax.dot_general(
            other_tokens, other, contract, preferred_element_type=jnp.float32
        )

    def slot_of(distance):
        owner = jnp.array(order, jnp.int32)[(pos - distance) % devices]
        return (blk - owner) % devices

    sequence = [0]
    for k in range(1, half):
        sequence += [k, -k]
    sequence.append(half)
    hidden = jnp.zeros(hidden_grad.shape, hidden_grad.dtype)
    grads = {}
    for d in sequence:
        if d == half:
            gate_other, up_other = partner(panels[d][0]), partner(panels[d][1])
        else:
            gate_other, up_other = partner(panels[d])
        gate, upper = rows(panels[d][0], gate_other), rows(panels[d][1], up_other)
        start = slot_of(d) * units
        incoming = lax.dynamic_slice_in_dim(hidden_grad, start, units, 1).astype(jnp.float32)
        sigma = jax.nn.sigmoid(gate)
        activated = gate * sigma
        hidden = lax.dynamic_update_slice_in_dim(hidden, (activated * upper).astype(jnp.bfloat16), start, 1)
        gate_grad = (incoming * upper * sigma * (1.0 + gate * (1.0 - sigma))).astype(jnp.bfloat16)
        up_grad = (incoming * activated).astype(jnp.bfloat16)
        grads[d] = (gate_grad, up_grad)

    def term(d, which):
        contract = (((0,), (0,)), ((), ()))
        away = lax.dot_general(grads[d][which], other_tokens, contract, preferred_element_type=jnp.float32)
        kept = lax.dot_general(grads[d][which], own_tokens, contract, preferred_element_type=jnp.float32)
        return kept + partner(away.astype(jnp.bfloat16)).astype(jnp.float32)

    def chain(sign):
        running = [None, None]
        lead = 0 if sign > 0 else 1
        running[lead] = term(half, lead)
        arrived = [None, None]
        arrived[lead] = hop(running[lead].astype(jnp.bfloat16), -sign)
        for k in range(half - 1, 0, -1):
            for which in range(2):
                running[which] = term(sign * k, which)
                if arrived[which] is not None:
                    running[which] = running[which] + arrived[which].astype(jnp.float32)
            arrived = [hop(value.astype(jnp.bfloat16), -sign) for value in running]
        return arrived

    up_way, down_way = chain(1), chain(-1)
    gradient = jnp.stack(
        [term(0, w) + up_way[w].astype(jnp.float32) + down_way[w].astype(jnp.float32) for w in range(2)]
    )
    norm_sq = lax.psum(jnp.sum(gradient * gradient), ("blk", "rep"))
    update = adam_update(
        joined(gradient, partner(gradient)),
        joined(first_moment, partner(first_moment)),
        joined(second_moment, partner(second_moment)),
        joined(weights, partner(weights)),
        norm_sq,
    )
    return (hidden, update)


def solution(mesh):
    placed = (
        P(("groups", "blk", "rep"), None),
        P(("groups", "blk", "rep"), None),
        P(None, "blk", "rep"),
        P(None, ("groups", "blk"), "rep"),
        P(None, ("groups", "blk"), "rep"),
    )
    devices = mesh.shape["blk"]

    def program(tokens, hidden_grad, weights, first_moment, second_moment):
        slots = hidden_grad.shape[1] * devices // weights.shape[1]
        whole_cycle = slots == devices and devices % 2 == 0 and devices >= 4 and mesh.shape["rep"] == 2
        step = jax.shard_map(
            on_ring if whole_cycle else on_device,
            mesh=mesh,
            in_specs=placed,
            out_specs=(P(("groups", "blk", "rep"), None), P(None, ("groups", "blk"), None)),
            check_vma=False,
        )
        return step(tokens, hidden_grad, weights, first_moment, second_moment)

    return program
```

```python
import functools

import jax
import jax.numpy as jnp
from jax import lax
from jax.experimental import pallas as pl
from jax.experimental.pallas import tpu as pltpu
from jax.sharding import PartitionSpec as P

clip_norm = 1.0
beta_one = 0.9
beta_two = 0.95
step_count = 10.0
adam_eps = 1e-08
decay_rate = 0.1


def shifted(value, axis, by):
    devices = lax.axis_size(axis)
    return lax.ppermute(value, axis, [(i, (i + by) % devices) for i in range(devices)])


def swiglu_terms(tokens, incoming_grad, gate_rows, up_rows):
    contract = (((1,), (1,)), ((), ()))
    gate = lax.dot_general(tokens, gate_rows, contract, preferred_element_type=jnp.float32)
    upper = lax.dot_general(tokens, up_rows, contract, preferred_element_type=jnp.float32)
    sigma = jax.nn.sigmoid(gate)
    activated = gate * sigma
    hidden = (activated * upper).astype(jnp.bfloat16)
    incoming = incoming_grad.astype(jnp.float32)
    gate_grad = (incoming * upper * sigma * (1.0 + gate * (1.0 - sigma))).astype(jnp.bfloat16)
    up_grad = (incoming * activated).astype(jnp.bfloat16)
    return (hidden, gate_grad, up_grad)


def adam_update(gradient, first_moment, second_moment, weights, norm_sq):
    clip_scale = jnp.minimum(1.0, clip_norm / jnp.sqrt(norm_sq))
    clipped = gradient * clip_scale
    first = beta_one * first_moment + (1.0 - beta_one) * clipped
    second = beta_two * second_moment + (1.0 - beta_two) * clipped * clipped
    first_hat = first / (1.0 - beta_one**step_count)
    second_hat = second / (1.0 - beta_two**step_count)
    return first_hat / (jnp.sqrt(second_hat) + adam_eps) + decay_rate * weights.astype(jnp.float32)


def on_device(tokens, hidden_grad, weights, first_moment, second_moment):
    unit_count = weights.shape[1]
    token_count = tokens.shape[0]
    slot_count = hidden_grad.shape[1] // unit_count
    own_full = lax.all_gather(weights, "rep", axis=2, tiled=True)
    slot_grads = jnp.swapaxes(hidden_grad.reshape(token_count, slot_count, unit_count), 0, 1)
    contract = (((1,), (0,)), ((), ()))

    def grad_term(gate_grad, up_grad):
        paired = jnp.stack([gate_grad, up_grad], axis=0)
        return lax.dot_general(paired, tokens, contract, preferred_element_type=jnp.float32)

    zero_sums = jnp.zeros((2, unit_count, tokens.shape[1]), jnp.float32)

    def visit(panel_rows, slot_grad):
        hidden, gate_grad, up_grad = swiglu_terms(tokens, slot_grad, panel_rows[0], panel_rows[1])
        arrived = shifted(panel_rows, "blk", 1)
        return (arrived, (hidden, gate_grad, up_grad))

    _, (hidden_slots, gate_slots, up_slots) = lax.scan(visit, own_full, slot_grads)

    def collect(running, grads_pair):
        arrived = shifted(running, "blk", -1)
        return (arrived + grad_term(grads_pair[0], grads_pair[1]), None)

    owned_sums, _ = lax.scan(collect, zero_sums, (gate_slots, up_slots), reverse=True)
    hidden = jnp.swapaxes(hidden_slots, 0, 1).reshape(token_count, slot_count * unit_count)
    gradient = lax.psum_scatter(owned_sums, "rep", scatter_dimension=2, tiled=True)
    norm_sq = lax.psum(jnp.sum(gradient * gradient), ("blk", "rep"))
    update = adam_update(gradient, first_moment, second_moment, weights, norm_sq)
    adam_step = lax.all_gather(update, "rep", axis=2, tiled=True)
    return (hidden, adam_step)


def total_kernel(devices, part_ref, out_ref, slots, send_sem, recv_sem):
    me = lax.axis_index("blk") * 2 + lax.axis_index("rep")

    def place(by):
        peer = (me + by) % devices
        return {"blk": peer // 2, "rep": peer % 2}

    barrier = pltpu.get_barrier_semaphore()
    for by in range(1, devices):
        pl.semaphore_signal(barrier, inc=1, device_id=place(by), device_id_type=pl.DeviceIdType.MESH)
    pl.semaphore_wait(barrier, devices - 1)
    slots[me] = part_ref[...]
    copies = []
    for by in range(1, devices):
        copy = pltpu.make_async_remote_copy(
            src_ref=part_ref,
            dst_ref=slots.at[me],
            send_sem=send_sem.at[by],
            recv_sem=recv_sem.at[by],
            device_id=place(by),
            device_id_type=pl.DeviceIdType.MESH,
        )
        copy.start()
        copies.append(copy)
    for copy in copies:
        copy.wait()
    total = slots[0]
    for i in range(1, devices):
        total = total + slots[i]
    out_ref[...] = total


def summed(value):
    devices = lax.axis_size("blk") * lax.axis_size("rep")
    return pl.pallas_call(
        functools.partial(total_kernel, devices),
        out_shape=jax.ShapeDtypeStruct((8, 128), jnp.float32),
        in_specs=[pl.BlockSpec(memory_space=pltpu.VMEM)],
        out_specs=pl.BlockSpec(memory_space=pltpu.VMEM),
        scratch_shapes=[
            pltpu.VMEM((devices, 8, 128), jnp.float32),
            pltpu.SemaphoreType.DMA((devices,)),
            pltpu.SemaphoreType.DMA((devices,)),
        ],
        compiler_params=pltpu.CompilerParams(collective_id=0, has_side_effects=True),
    )(jnp.broadcast_to(value, (8, 128)))


def adam_kernel(norm_ref, *refs):
    own, other, out_ref = refs[:4], refs[4:8], refs[8]
    features = own[0].shape[-1]
    norm_sq = norm_ref[0:1, 0:1]

    def write(values, first):
        gradient, first_moment, second_moment, weights = (ref[0] for ref in values)
        out_ref[0, :, first : first + features] = adam_update(
            gradient, first_moment, second_moment, weights, norm_sq
        )

    rep = lax.axis_index("rep")

    @pl.when(rep == 0)
    def _():
        write(own, 0)
        write(other, features)

    @pl.when(rep != 0)
    def _():
        write(other, 0)
        write(own, features)


def adam_all(norm_sq, own, other):
    pair, units, features = own[0].shape
    tile = min(units, 128)
    block = pl.BlockSpec((1, tile, features), lambda i, j: (i, j, 0))
    return pl.pallas_call(
        adam_kernel,
        grid=(pair, units // tile),
        out_shape=jax.ShapeDtypeStruct((pair, units, 2 * features), jnp.float32),
        in_specs=[pl.BlockSpec((8, 128), lambda i, j: (0, 0))] + [block] * 8,
        out_specs=pl.BlockSpec((1, tile, 2 * features), lambda i, j: (i, j, 0)),
        compiler_params=pltpu.CompilerParams(vmem_limit_bytes=24 * 1024 * 1024),
    )(norm_sq, *own, *other)


def ring_order(devices):
    return list(range(0, devices, 2)) + list(range(devices - 1, 0, -2))


def on_ring(tokens, hidden_grad, weights, first_moment, second_moment):
    devices = lax.axis_size("blk")
    half = devices // 2
    units, features = weights.shape[1], weights.shape[2]
    order = ring_order(devices)
    blk, rep = lax.axis_index("blk"), lax.axis_index("rep")
    positions = [order.index(i) for i in range(devices)]
    pos = jnp.array(positions, jnp.int32)[blk]

    def hop(value, by):
        return lax.ppermute(value, "blk", [(order[i], order[(i + by) % devices]) for i in range(devices)])

    def partner(value):
        return lax.ppermute(value, "rep", [(0, 1), (1, 0)])

    own_tokens = lax.dynamic_slice_in_dim(tokens, rep * features, features, 1)
    other_tokens = lax.dynamic_slice_in_dim(tokens, (1 - rep) * features, features, 1)

    panels = {0: weights}
    for k in range(1, half):
        panels[k] = hop(panels[k - 1], 1)
        panels[-k] = hop(panels[1 - k], -1)
    panels[half] = (hop(panels[half - 1][0], 1), hop(panels[1 - half][1], -1))

    def rows(own, other):
        contract = (((1,), (1,)), ((), ()))
        return lax.dot_general(own_tokens, own, contract, preferred_element_type=jnp.float32) + lax.dot_general(
            other_tokens, other, contract, preferred_element_type=jnp.float32
        )

    def slot_of(distance):
        owner = jnp.array(order, jnp.int32)[(pos - distance) % devices]
        return (blk - owner) % devices

    sequence = [0]
    for k in range(1, half):
        sequence += [k, -k]
    sequence.append(half)
    hidden = jnp.zeros(hidden_grad.shape, hidden_grad.dtype)
    grads = {}
    for d in sequence:
        if d == half:
            gate_other, up_other = partner(panels[d][0]), partner(panels[d][1])
        else:
            gate_other, up_other = partner(panels[d])
        gate, upper = rows(panels[d][0], gate_other), rows(panels[d][1], up_other)
        start = slot_of(d) * units
        incoming = lax.dynamic_slice_in_dim(hidden_grad, start, units, 1).astype(jnp.float32)
        sigma = jax.nn.sigmoid(gate)
        activated = gate * sigma
        hidden = lax.dynamic_update_slice_in_dim(hidden, (activated * upper).astype(jnp.bfloat16), start, 1)
        gate_grad = (incoming * upper * sigma * (1.0 + gate * (1.0 - sigma))).astype(jnp.bfloat16)
        up_grad = (incoming * activated).astype(jnp.bfloat16)
        grads[d] = (gate_grad, up_grad)

    def term(d, which):
        contract = (((0,), (0,)), ((), ()))
        away = lax.dot_general(grads[d][which], other_tokens, contract, preferred_element_type=jnp.float32)
        kept = lax.dot_general(grads[d][which], own_tokens, contract, preferred_element_type=jnp.float32)
        return kept + partner(away.astype(jnp.bfloat16)).astype(jnp.float32)

    def chain(sign):
        running = [None, None]
        lead = 0 if sign > 0 else 1
        running[lead] = term(half, lead)
        arrived = [None, None]
        arrived[lead] = hop(running[lead].astype(jnp.bfloat16), -sign)
        for k in range(half - 1, 0, -1):
            for which in range(2):
                running[which] = term(sign * k, which)
                if arrived[which] is not None:
                    running[which] = running[which] + arrived[which].astype(jnp.float32)
            arrived = [hop(value.astype(jnp.bfloat16), -sign) for value in running]
        return arrived

    up_way, down_way = chain(1), chain(-1)
    gradient = jnp.stack(
        [term(0, w) + up_way[w].astype(jnp.float32) + down_way[w].astype(jnp.float32) for w in range(2)]
    )
    norm_sq = summed(jnp.sum(gradient * gradient))
    own = (gradient, first_moment, second_moment, weights)
    update = adam_all(norm_sq, own, tuple(partner(value) for value in own))
    return (hidden, update)


def solution(mesh):
    placed = (
        P(("groups", "blk", "rep"), None),
        P(("groups", "blk", "rep"), None),
        P(None, "blk", "rep"),
        P(None, ("groups", "blk"), "rep"),
        P(None, ("groups", "blk"), "rep"),
    )
    devices = mesh.shape["blk"]

    def program(tokens, hidden_grad, weights, first_moment, second_moment):
        slots = hidden_grad.shape[1] * devices // weights.shape[1]
        whole_cycle = slots == devices and devices % 2 == 0 and devices >= 4 and mesh.shape["rep"] == 2
        step = jax.shard_map(
            on_ring if whole_cycle else on_device,
            mesh=mesh,
            in_specs=placed,
            out_specs=(P(("groups", "blk", "rep"), None), P(None, ("groups", "blk"), None)),
            check_vma=False,
        )
        return step(tokens, hidden_grad, weights, first_moment, second_moment)

    return program
```

```python
import functools

import jax
import jax.numpy as jnp
from jax import lax
from jax.experimental import pallas as pl
from jax.experimental.pallas import tpu as pltpu
from jax.sharding import PartitionSpec as P

clip_norm = 1.0
beta_one = 0.9
beta_two = 0.95
step_count = 10.0
adam_eps = 1e-08
decay_rate = 0.1


def shifted(value, axis, by):
    devices = lax.axis_size(axis)
    return lax.ppermute(value, axis, [(i, (i + by) % devices) for i in range(devices)])


def swiglu_terms(tokens, incoming_grad, gate_rows, up_rows):
    contract = (((1,), (1,)), ((), ()))
    gate = lax.dot_general(tokens, gate_rows, contract, preferred_element_type=jnp.float32)
    upper = lax.dot_general(tokens, up_rows, contract, preferred_element_type=jnp.float32)
    sigma = jax.nn.sigmoid(gate)
    activated = gate * sigma
    hidden = (activated * upper).astype(jnp.bfloat16)
    incoming = incoming_grad.astype(jnp.float32)
    gate_grad = (incoming * upper * sigma * (1.0 + gate * (1.0 - sigma))).astype(jnp.bfloat16)
    up_grad = (incoming * activated).astype(jnp.bfloat16)
    return (hidden, gate_grad, up_grad)


def adam_update(gradient, first_moment, second_moment, weights, norm_sq):
    clip_scale = jnp.minimum(1.0, clip_norm / jnp.sqrt(norm_sq))
    clipped = gradient * clip_scale
    first = beta_one * first_moment + (1.0 - beta_one) * clipped
    second = beta_two * second_moment + (1.0 - beta_two) * clipped * clipped
    first_hat = first / (1.0 - beta_one**step_count)
    second_hat = second / (1.0 - beta_two**step_count)
    return first_hat / (jnp.sqrt(second_hat) + adam_eps) + decay_rate * weights.astype(jnp.float32)


def on_device(tokens, hidden_grad, weights, first_moment, second_moment):
    unit_count = weights.shape[1]
    token_count = tokens.shape[0]
    slot_count = hidden_grad.shape[1] // unit_count
    own_full = lax.all_gather(weights, "rep", axis=2, tiled=True)
    slot_grads = jnp.swapaxes(hidden_grad.reshape(token_count, slot_count, unit_count), 0, 1)
    contract = (((1,), (0,)), ((), ()))

    def grad_term(gate_grad, up_grad):
        paired = jnp.stack([gate_grad, up_grad], axis=0)
        return lax.dot_general(paired, tokens, contract, preferred_element_type=jnp.float32)

    zero_sums = jnp.zeros((2, unit_count, tokens.shape[1]), jnp.float32)

    def visit(panel_rows, slot_grad):
        hidden, gate_grad, up_grad = swiglu_terms(tokens, slot_grad, panel_rows[0], panel_rows[1])
        arrived = shifted(panel_rows, "blk", 1)
        return (arrived, (hidden, gate_grad, up_grad))

    _, (hidden_slots, gate_slots, up_slots) = lax.scan(visit, own_full, slot_grads)

    def collect(running, grads_pair):
        arrived = shifted(running, "blk", -1)
        return (arrived + grad_term(grads_pair[0], grads_pair[1]), None)

    owned_sums, _ = lax.scan(collect, zero_sums, (gate_slots, up_slots), reverse=True)
    hidden = jnp.swapaxes(hidden_slots, 0, 1).reshape(token_count, slot_count * unit_count)
    gradient = lax.psum_scatter(owned_sums, "rep", scatter_dimension=2, tiled=True)
    norm_sq = lax.psum(jnp.sum(gradient * gradient), ("blk", "rep"))
    update = adam_update(gradient, first_moment, second_moment, weights, norm_sq)
    adam_step = lax.all_gather(update, "rep", axis=2, tiled=True)
    return (hidden, adam_step)


def total_kernel(devices, part_ref, out_ref, slots, send_sem, recv_sem):
    me = lax.axis_index("blk") * 2 + lax.axis_index("rep")

    def place(by):
        peer = (me + by) % devices
        return {"blk": peer // 2, "rep": peer % 2}

    barrier = pltpu.get_barrier_semaphore()
    for by in range(1, devices):
        pl.semaphore_signal(barrier, inc=1, device_id=place(by), device_id_type=pl.DeviceIdType.MESH)
    pl.semaphore_wait(barrier, devices - 1)
    slots[me] = part_ref[...]
    copies = []
    for by in range(1, devices):
        copy = pltpu.make_async_remote_copy(
            src_ref=part_ref,
            dst_ref=slots.at[me],
            send_sem=send_sem.at[by],
            recv_sem=recv_sem.at[by],
            device_id=place(by),
            device_id_type=pl.DeviceIdType.MESH,
        )
        copy.start()
        copies.append(copy)
    for copy in copies:
        copy.wait()
    total = slots[0]
    for i in range(1, devices):
        total = total + slots[i]
    out_ref[...] = total


def summed(value):
    devices = lax.axis_size("blk") * lax.axis_size("rep")
    return pl.pallas_call(
        functools.partial(total_kernel, devices),
        out_shape=jax.ShapeDtypeStruct((8, 128), jnp.float32),
        in_specs=[pl.BlockSpec(memory_space=pltpu.VMEM)],
        out_specs=pl.BlockSpec(memory_space=pltpu.VMEM),
        scratch_shapes=[
            pltpu.VMEM((devices, 8, 128), jnp.float32),
            pltpu.SemaphoreType.DMA((devices,)),
            pltpu.SemaphoreType.DMA((devices,)),
        ],
        compiler_params=pltpu.CompilerParams(collective_id=0, has_side_effects=True),
    )(jnp.broadcast_to(value, (8, 128)))


def adam_kernel(norm_ref, *refs):
    own, other, out_ref = refs[:4], refs[4:8], refs[8]
    features = own[0].shape[-1]
    norm_sq = norm_ref[0:1, 0:1]

    def write(values, first):
        gradient, first_moment, second_moment, weights = (ref[0] for ref in values)
        out_ref[0, :, first : first + features] = adam_update(
            gradient, first_moment, second_moment, weights, norm_sq
        )

    rep = lax.axis_index("rep")

    @pl.when(rep == 0)
    def _():
        write(own, 0)
        write(other, features)

    @pl.when(rep != 0)
    def _():
        write(other, 0)
        write(own, features)


def adam_all(norm_sq, own, other):
    pair, units, features = own[0].shape
    tile = min(units, 128)
    block = pl.BlockSpec((1, tile, features), lambda i, j: (i, j, 0))
    return pl.pallas_call(
        adam_kernel,
        grid=(pair, units // tile),
        out_shape=jax.ShapeDtypeStruct((pair, units, 2 * features), jnp.float32),
        in_specs=[pl.BlockSpec((8, 128), lambda i, j: (0, 0))] + [block] * 8,
        out_specs=pl.BlockSpec((1, tile, 2 * features), lambda i, j: (i, j, 0)),
        compiler_params=pltpu.CompilerParams(vmem_limit_bytes=24 * 1024 * 1024),
    )(norm_sq, *own, *other)


def gather_kernel(
    cross, tokens_ref, grad_ref, weights_ref, hidden_ref, out_grads_ref, mine, other, ring_send, ring_recv,
    cross_send, cross_recv, near_send, near_recv, far_send, far_recv
):
    devices = lax.axis_size("blk")
    half = devices // 2
    units, features = weights_ref.shape[1], weights_ref.shape[2]
    token_count = tokens_ref.shape[0]
    blk, rep, group = lax.axis_index("blk"), lax.axis_index("rep"), lax.axis_index("groups")
    parity = blk % 2
    pos = (1 - parity) * (blk // 2) + parity * (devices - 1 - blk // 2)

    def at_position(q):
        late = q // half
        return (1 - late) * 2 * q + late * (2 * (devices - 1 - q) + 1)

    after = {"blk": at_position((pos + 1) % devices)}
    before = {"blk": at_position((pos + devices - 1) % devices)}
    near = {"rep": 1 - rep}
    across = {"groups": 1 - group}
    mesh_ids = pl.DeviceIdType.MESH

    ring_rows = units - cross
    ring_at = pl.multiple_of((1 - group) * cross, 16)
    give_at = pl.multiple_of((1 - group) * ring_rows, 16)
    take_at = pl.multiple_of(group * ring_rows, 16)
    whole, ring_part = pl.ds(0, units), pl.ds(ring_at, ring_rows)
    give_part, take_part = pl.ds(give_at, cross), pl.ds(take_at, cross)

    def index_of(direction, k):
        if k == half:
            return devices - 1
        return k if direction > 0 else half - 1 + k

    barrier = pltpu.get_barrier_semaphore()
    for peer in (after, before, near, across):
        pl.semaphore_signal(barrier, inc=1, device_id=peer, device_id_type=mesh_ids)
    pl.semaphore_wait(barrier, 4)

    started = []

    def send(source, target, part, send_sem, recv_sem, peer):
        copy = pltpu.make_async_remote_copy(
            src_ref=source.at[part], dst_ref=target.at[part], send_sem=send_sem, recv_sem=recv_sem,
            device_id=peer, device_id_type=mesh_ids,
        )
        copy.start()
        started.append(copy)

    def arrive(target, part, send_sem, recv_sem, peer):
        pltpu.make_async_remote_copy(
            src_ref=target.at[part], dst_ref=target.at[part], send_sem=send_sem, recv_sem=recv_sem,
            device_id=peer, device_id_type=mesh_ids,
        ).wait_recv()

    def forward(direction, k, which):
        if k + 1 == half and which != (0 if direction > 0 else 1):
            return
        source = weights_ref.at[which] if k == 0 else mine.at[index_of(direction, k), which]
        to = index_of(direction, k + 1)
        send(
            source, mine.at[to, which], ring_part, ring_send.at[to, which], ring_recv.at[to, which],
            after if direction > 0 else before,
        )

    def ring_step(direction, k, which):
        i = index_of(direction, k)
        arrive(mine.at[i, which], ring_part, ring_send.at[i, which], ring_recv.at[i, which], after)
        if k < half:
            forward(direction, k, which)
        send(mine.at[i, which], mine.at[i, which], give_part, cross_send.at[i, which], cross_recv.at[i, which], across)
        send(mine.at[i, which], other.at[i, which], ring_part, near_send.at[i, which], near_recv.at[i, which], near)

    def complete(i):
        for which in range(2):
            arrive(mine.at[i, which], take_part, cross_send.at[i, which], cross_recv.at[i, which], across)
            send(mine.at[i, which], other.at[i, which], take_part, far_send.at[i, which], far_recv.at[i, which], near)
        for which in range(2):
            arrive(other.at[i, which], ring_part, near_send.at[i, which], near_recv.at[i, which], near)
            arrive(other.at[i, which], take_part, far_send.at[i, which], far_recv.at[i, which], near)

    own_at = pl.multiple_of(rep * features, 128)
    other_at = pl.multiple_of((1 - rep) * features, 128)
    tile = min(token_count, 256)
    contract = (((1,), (1,)), ((), ()))

    def compute(i, signed):
        owner = at_position((pos - signed + devices) % devices)
        slot = (blk - owner + devices) % devices
        columns = pl.ds(pl.multiple_of(slot * units, 128), units)

        @pl.loop(0, token_count // tile)
        def _(t):
            rows = pl.ds(pl.multiple_of(t * tile, tile), tile)
            own_tokens = tokens_ref[rows, pl.ds(own_at, features)]
            other_tokens = tokens_ref[rows, pl.ds(other_at, features)]

            def product(which):
                own = weights_ref[which] if i == 0 else mine[i, which]
                return lax.dot_general(own_tokens, own, contract, preferred_element_type=jnp.float32) + lax.dot_general(
                    other_tokens, other[i, which], contract, preferred_element_type=jnp.float32
                )

            gate, upper = product(0), product(1)
            incoming = grad_ref[rows, columns].astype(jnp.float32)
            sigma = jax.nn.sigmoid(gate)
            activated = gate * sigma
            hidden_ref[rows, columns] = (activated * upper).astype(jnp.bfloat16)
            out_grads_ref[i, 0, rows, :] = (incoming * upper * sigma * (1.0 + gate * (1.0 - sigma))).astype(jnp.bfloat16)
            out_grads_ref[i, 1, rows, :] = (incoming * activated).astype(jnp.bfloat16)

    for which in range(2):
        for direction in (1, -1):
            forward(direction, 0, which)
    for which in range(2):
        send(weights_ref.at[which], other.at[0, which], whole, near_send.at[0, which], near_recv.at[0, which], near)
    for which in range(2):
        arrive(other.at[0, which], whole, near_send.at[0, which], near_recv.at[0, which], near)
    compute(0, 0)
    for k in range(1, half):
        for which, side in ((0, 1), (1, -1)):
            for direction in (1, -1):
                ring_step(direction, k, which)
            if k > 1:
                complete(index_of(side, k - 1))
                compute(index_of(side, k - 1), side * (k - 1))
    for which, side in ((0, 1), (1, -1)):
        ring_step(side, half, which)
        complete(index_of(side, half - 1))
        compute(index_of(side, half - 1), side * (half - 1))
    complete(devices - 1)
    compute(devices - 1, half)
    for copy in started:
        copy.wait_send()


def gathered_forward(tokens, hidden_grad, weights):
    devices = lax.axis_size("blk")
    units, features = weights.shape[1], weights.shape[2]
    cross = max(16, (units * 5 // 16) // 16 * 16)
    vmem = pl.BlockSpec(memory_space=pltpu.VMEM)
    sems = pltpu.SemaphoreType.DMA((devices, 2))
    return pl.pallas_call(
        functools.partial(gather_kernel, cross),
        out_shape=(
            jax.ShapeDtypeStruct(hidden_grad.shape, jnp.bfloat16),
            jax.ShapeDtypeStruct((devices, 2, tokens.shape[0], units), jnp.bfloat16),
        ),
        in_specs=[vmem] * 3,
        out_specs=(vmem, vmem),
        scratch_shapes=[
            pltpu.VMEM((devices, 2, units, features), jnp.bfloat16),
            pltpu.VMEM((devices, 2, units, features), jnp.bfloat16),
        ]
        + [sems] * 8,
        compiler_params=pltpu.CompilerParams(
            collective_id=1, has_side_effects=True, vmem_limit_bytes=56 * 1024 * 1024
        ),
    )(tokens, hidden_grad, weights)


def ring_order(devices):
    return list(range(0, devices, 2)) + list(range(devices - 1, 0, -2))


def on_ring(tokens, hidden_grad, weights, first_moment, second_moment):
    devices = lax.axis_size("blk")
    half = devices // 2
    features = weights.shape[2]
    order = ring_order(devices)
    rep = lax.axis_index("rep")

    def hop(value, by):
        return lax.ppermute(value, "blk", [(order[i], order[(i + by) % devices]) for i in range(devices)])

    def partner(value):
        return lax.ppermute(value, "rep", [(0, 1), (1, 0)])

    own_tokens = lax.dynamic_slice_in_dim(tokens, rep * features, features, 1)
    other_tokens = lax.dynamic_slice_in_dim(tokens, (1 - rep) * features, features, 1)

    hidden, slot_grads = gathered_forward(tokens, hidden_grad, weights)

    def index_of(d):
        return d if d >= 0 and d < half else (devices - 1 if d == half else half - 1 - d)

    grads = {d: slot_grads[index_of(d)] for d in range(1 - half, half + 1)}

    def term(d, which):
        contract = (((0,), (0,)), ((), ()))
        away = lax.dot_general(grads[d][which], other_tokens, contract, preferred_element_type=jnp.float32)
        kept = lax.dot_general(grads[d][which], own_tokens, contract, preferred_element_type=jnp.float32)
        return kept + partner(away.astype(jnp.bfloat16)).astype(jnp.float32)

    def chain(sign):
        running = [None, None]
        lead = 0 if sign > 0 else 1
        running[lead] = term(half, lead)
        arrived = [None, None]
        arrived[lead] = hop(running[lead].astype(jnp.bfloat16), -sign)
        for k in range(half - 1, 0, -1):
            for which in range(2):
                running[which] = term(sign * k, which)
                if arrived[which] is not None:
                    running[which] = running[which] + arrived[which].astype(jnp.float32)
            arrived = [hop(value.astype(jnp.bfloat16), -sign) for value in running]
        return arrived

    up_way, down_way = chain(1), chain(-1)
    gradient = jnp.stack(
        [term(0, w) + up_way[w].astype(jnp.float32) + down_way[w].astype(jnp.float32) for w in range(2)]
    )
    norm_sq = summed(jnp.sum(gradient * gradient))
    own = (gradient, first_moment, second_moment, weights)
    update = adam_all(norm_sq, own, tuple(partner(value) for value in own))
    return (hidden, update)


def solution(mesh):
    placed = (
        P(("groups", "blk", "rep"), None),
        P(("groups", "blk", "rep"), None),
        P(None, "blk", "rep"),
        P(None, ("groups", "blk"), "rep"),
        P(None, ("groups", "blk"), "rep"),
    )
    devices = mesh.shape["blk"]

    def program(tokens, hidden_grad, weights, first_moment, second_moment):
        slots = hidden_grad.shape[1] * devices // weights.shape[1]
        whole_cycle = slots == devices and devices % 2 == 0 and devices >= 4 and mesh.shape["rep"] == 2 and mesh.shape["groups"] == 2
        step = jax.shard_map(
            on_ring if whole_cycle else on_device,
            mesh=mesh,
            in_specs=placed,
            out_specs=(P(("groups", "blk", "rep"), None), P(None, ("groups", "blk"), None)),
            check_vma=False,
        )
        return step(tokens, hidden_grad, weights, first_moment, second_moment)

    return program
```

```python
import functools

import jax
import jax.numpy as jnp
from jax import lax
from jax.experimental import pallas as pl
from jax.experimental.pallas import tpu as pltpu
from jax.sharding import PartitionSpec as P

clip_norm = 1.0
beta_one = 0.9
beta_two = 0.95
step_count = 10.0
adam_eps = 1e-08
decay_rate = 0.1


def shifted(value, axis, by):
    devices = lax.axis_size(axis)
    return lax.ppermute(value, axis, [(i, (i + by) % devices) for i in range(devices)])


def swiglu_terms(tokens, incoming_grad, gate_rows, up_rows):
    contract = (((1,), (1,)), ((), ()))
    gate = lax.dot_general(tokens, gate_rows, contract, preferred_element_type=jnp.float32)
    upper = lax.dot_general(tokens, up_rows, contract, preferred_element_type=jnp.float32)
    sigma = jax.nn.sigmoid(gate)
    activated = gate * sigma
    hidden = (activated * upper).astype(jnp.bfloat16)
    incoming = incoming_grad.astype(jnp.float32)
    gate_grad = (incoming * upper * sigma * (1.0 + gate * (1.0 - sigma))).astype(jnp.bfloat16)
    up_grad = (incoming * activated).astype(jnp.bfloat16)
    return (hidden, gate_grad, up_grad)


def adam_update(gradient, first_moment, second_moment, weights, norm_sq):
    clip_scale = jnp.minimum(1.0, clip_norm / jnp.sqrt(norm_sq))
    clipped = gradient * clip_scale
    first = beta_one * first_moment + (1.0 - beta_one) * clipped
    second = beta_two * second_moment + (1.0 - beta_two) * clipped * clipped
    first_hat = first / (1.0 - beta_one**step_count)
    second_hat = second / (1.0 - beta_two**step_count)
    return first_hat / (jnp.sqrt(second_hat) + adam_eps) + decay_rate * weights.astype(jnp.float32)


def on_device(tokens, hidden_grad, weights, first_moment, second_moment):
    unit_count = weights.shape[1]
    token_count = tokens.shape[0]
    slot_count = hidden_grad.shape[1] // unit_count
    own_full = lax.all_gather(weights, "rep", axis=2, tiled=True)
    slot_grads = jnp.swapaxes(hidden_grad.reshape(token_count, slot_count, unit_count), 0, 1)
    contract = (((1,), (0,)), ((), ()))

    def grad_term(gate_grad, up_grad):
        paired = jnp.stack([gate_grad, up_grad], axis=0)
        return lax.dot_general(paired, tokens, contract, preferred_element_type=jnp.float32)

    zero_sums = jnp.zeros((2, unit_count, tokens.shape[1]), jnp.float32)

    def visit(panel_rows, slot_grad):
        hidden, gate_grad, up_grad = swiglu_terms(tokens, slot_grad, panel_rows[0], panel_rows[1])
        arrived = shifted(panel_rows, "blk", 1)
        return (arrived, (hidden, gate_grad, up_grad))

    _, (hidden_slots, gate_slots, up_slots) = lax.scan(visit, own_full, slot_grads)

    def collect(running, grads_pair):
        arrived = shifted(running, "blk", -1)
        return (arrived + grad_term(grads_pair[0], grads_pair[1]), None)

    owned_sums, _ = lax.scan(collect, zero_sums, (gate_slots, up_slots), reverse=True)
    hidden = jnp.swapaxes(hidden_slots, 0, 1).reshape(token_count, slot_count * unit_count)
    gradient = lax.psum_scatter(owned_sums, "rep", scatter_dimension=2, tiled=True)
    norm_sq = lax.psum(jnp.sum(gradient * gradient), ("blk", "rep"))
    update = adam_update(gradient, first_moment, second_moment, weights, norm_sq)
    adam_step = lax.all_gather(update, "rep", axis=2, tiled=True)
    return (hidden, adam_step)


def total_kernel(devices, part_ref, out_ref, slots, send_sem, recv_sem):
    me = lax.axis_index("blk") * 2 + lax.axis_index("rep")

    def place(by):
        peer = (me + by) % devices
        return {"blk": peer // 2, "rep": peer % 2}

    barrier = pltpu.get_barrier_semaphore()
    for by in range(1, devices):
        pl.semaphore_signal(barrier, inc=1, device_id=place(by), device_id_type=pl.DeviceIdType.MESH)
    pl.semaphore_wait(barrier, devices - 1)
    slots[me] = part_ref[...]
    copies = []
    for by in range(1, devices):
        copy = pltpu.make_async_remote_copy(
            src_ref=part_ref,
            dst_ref=slots.at[me],
            send_sem=send_sem.at[by],
            recv_sem=recv_sem.at[by],
            device_id=place(by),
            device_id_type=pl.DeviceIdType.MESH,
        )
        copy.start()
        copies.append(copy)
    for copy in copies:
        copy.wait()
    total = slots[0]
    for i in range(1, devices):
        total = total + slots[i]
    out_ref[...] = total


def summed(value):
    devices = lax.axis_size("blk") * lax.axis_size("rep")
    return pl.pallas_call(
        functools.partial(total_kernel, devices),
        out_shape=jax.ShapeDtypeStruct((8, 128), jnp.float32),
        in_specs=[pl.BlockSpec(memory_space=pltpu.VMEM)],
        out_specs=pl.BlockSpec(memory_space=pltpu.VMEM),
        scratch_shapes=[
            pltpu.VMEM((devices, 8, 128), jnp.float32),
            pltpu.SemaphoreType.DMA((devices,)),
            pltpu.SemaphoreType.DMA((devices,)),
        ],
        compiler_params=pltpu.CompilerParams(collective_id=0, has_side_effects=True),
    )(jnp.broadcast_to(value, (8, 128)))


def adam_kernel(norm_ref, *refs):
    own, other, out_ref = refs[:4], refs[4:8], refs[8]
    features = own[0].shape[-1]
    norm_sq = norm_ref[0:1, 0:1]

    def write(values, first):
        gradient, first_moment, second_moment, weights = (ref[0] for ref in values)
        out_ref[0, :, first : first + features] = adam_update(
            gradient, first_moment, second_moment, weights, norm_sq
        )

    rep = lax.axis_index("rep")

    @pl.when(rep == 0)
    def _():
        write(own, 0)
        write(other, features)

    @pl.when(rep != 0)
    def _():
        write(other, 0)
        write(own, features)


def adam_all(norm_sq, own, other):
    pair, units, features = own[0].shape
    tile = min(units, 128)
    block = pl.BlockSpec((1, tile, features), lambda i, j: (i, j, 0))
    return pl.pallas_call(
        adam_kernel,
        grid=(pair, units // tile),
        out_shape=jax.ShapeDtypeStruct((pair, units, 2 * features), jnp.float32),
        in_specs=[pl.BlockSpec((8, 128), lambda i, j: (0, 0))] + [block] * 8,
        out_specs=pl.BlockSpec((1, tile, 2 * features), lambda i, j: (i, j, 0)),
        compiler_params=pltpu.CompilerParams(vmem_limit_bytes=24 * 1024 * 1024),
    )(norm_sq, *own, *other)


def gather_kernel(
    cross, tokens_ref, grad_ref, weights_ref, hidden_ref, out_grads_ref, mine, other, ring_send, ring_recv,
    cross_send, cross_recv, near_send, near_recv, far_send, far_recv
):
    devices = lax.axis_size("blk")
    half = devices // 2
    units, features = weights_ref.shape[1], weights_ref.shape[2]
    token_count = tokens_ref.shape[0]
    blk, rep, group = lax.axis_index("blk"), lax.axis_index("rep"), lax.axis_index("groups")
    parity = blk % 2
    pos = (1 - parity) * (blk // 2) + parity * (devices - 1 - blk // 2)

    def at_position(q):
        late = q // half
        return (1 - late) * 2 * q + late * (2 * (devices - 1 - q) + 1)

    after = {"blk": at_position((pos + 1) % devices)}
    before = {"blk": at_position((pos + devices - 1) % devices)}
    near = {"rep": 1 - rep}
    across = {"groups": 1 - group}
    mesh_ids = pl.DeviceIdType.MESH

    ring_rows = units - cross
    ring_at = pl.multiple_of((1 - group) * cross, 16)
    give_at = pl.multiple_of((1 - group) * ring_rows, 16)
    take_at = pl.multiple_of(group * ring_rows, 16)
    whole, ring_part = pl.ds(0, units), pl.ds(ring_at, ring_rows)
    give_part, take_part = pl.ds(give_at, cross), pl.ds(take_at, cross)

    def index_of(direction, k):
        if k == half:
            return devices - 1
        return k if direction > 0 else half - 1 + k

    barrier = pltpu.get_barrier_semaphore()
    for peer in (after, before, near, across):
        pl.semaphore_signal(barrier, inc=1, device_id=peer, device_id_type=mesh_ids)
    pl.semaphore_wait(barrier, 4)

    started = []

    def send(source, target, part, send_sem, recv_sem, peer):
        copy = pltpu.make_async_remote_copy(
            src_ref=source.at[part], dst_ref=target.at[part], send_sem=send_sem, recv_sem=recv_sem,
            device_id=peer, device_id_type=mesh_ids,
        )
        copy.start()
        started.append(copy)

    def arrive(target, part, send_sem, recv_sem, peer):
        pltpu.make_async_remote_copy(
            src_ref=target.at[part], dst_ref=target.at[part], send_sem=send_sem, recv_sem=recv_sem,
            device_id=peer, device_id_type=mesh_ids,
        ).wait_recv()

    def forward(direction, k, which):
        if k + 1 == half and which != (0 if direction > 0 else 1):
            return
        source = weights_ref.at[which] if k == 0 else mine.at[index_of(direction, k), which]
        to = index_of(direction, k + 1)
        send(
            source, mine.at[to, which], ring_part, ring_send.at[to, which], ring_recv.at[to, which],
            after if direction > 0 else before,
        )

    def ring_step(direction, k, which):
        i = index_of(direction, k)
        arrive(mine.at[i, which], ring_part, ring_send.at[i, which], ring_recv.at[i, which], after)
        if k < half:
            forward(direction, k, which)
        send(mine.at[i, which], mine.at[i, which], give_part, cross_send.at[i, which], cross_recv.at[i, which], across)
        send(mine.at[i, which], other.at[i, which], ring_part, near_send.at[i, which], near_recv.at[i, which], near)

    def complete(i):
        for which in range(2):
            arrive(mine.at[i, which], take_part, cross_send.at[i, which], cross_recv.at[i, which], across)
            send(mine.at[i, which], other.at[i, which], take_part, far_send.at[i, which], far_recv.at[i, which], near)
        for which in range(2):
            arrive(other.at[i, which], ring_part, near_send.at[i, which], near_recv.at[i, which], near)
            arrive(other.at[i, which], take_part, far_send.at[i, which], far_recv.at[i, which], near)

    own_at = pl.multiple_of(rep * features, 128)
    other_at = pl.multiple_of((1 - rep) * features, 128)
    tile = min(token_count, 256)
    contract = (((1,), (1,)), ((), ()))

    def compute(i, signed):
        owner = at_position((pos - signed + devices) % devices)
        slot = (blk - owner + devices) % devices
        columns = pl.ds(pl.multiple_of(slot * units, 128), units)

        @pl.loop(0, token_count // tile)
        def _(t):
            rows = pl.ds(pl.multiple_of(t * tile, tile), tile)
            own_tokens = tokens_ref[rows, pl.ds(own_at, features)]
            other_tokens = tokens_ref[rows, pl.ds(other_at, features)]

            def product(which):
                own = weights_ref[which] if i == 0 else mine[i, which]
                return lax.dot_general(own_tokens, own, contract, preferred_element_type=jnp.float32) + lax.dot_general(
                    other_tokens, other[i, which], contract, preferred_element_type=jnp.float32
                )

            gate, upper = product(0), product(1)
            incoming = grad_ref[rows, columns].astype(jnp.float32)
            sigma = jax.nn.sigmoid(gate)
            activated = gate * sigma
            hidden_ref[rows, columns] = (activated * upper).astype(jnp.bfloat16)
            out_grads_ref[i, 0, rows, :] = (incoming * upper * sigma * (1.0 + gate * (1.0 - sigma))).astype(jnp.bfloat16)
            out_grads_ref[i, 1, rows, :] = (incoming * activated).astype(jnp.bfloat16)

    for which in range(2):
        for direction in (1, -1):
            forward(direction, 0, which)
    for which in range(2):
        send(weights_ref.at[which], other.at[0, which], whole, near_send.at[0, which], near_recv.at[0, which], near)
    for which in range(2):
        arrive(other.at[0, which], whole, near_send.at[0, which], near_recv.at[0, which], near)
    compute(0, 0)
    for k in range(1, half):
        for which, side in ((0, 1), (1, -1)):
            for direction in (1, -1):
                ring_step(direction, k, which)
            if k > 1:
                complete(index_of(side, k - 1))
                compute(index_of(side, k - 1), side * (k - 1))
    for which, side in ((0, 1), (1, -1)):
        ring_step(side, half, which)
        complete(index_of(side, half - 1))
        compute(index_of(side, half - 1), side * (half - 1))
    complete(devices - 1)
    compute(devices - 1, half)
    for copy in started:
        copy.wait_send()


def gathered_forward(tokens, hidden_grad, weights):
    devices = lax.axis_size("blk")
    units, features = weights.shape[1], weights.shape[2]
    cross = max(16, (units * 5 // 16) // 16 * 16)
    vmem = pl.BlockSpec(memory_space=pltpu.VMEM)
    sems = pltpu.SemaphoreType.DMA((devices, 2))
    return pl.pallas_call(
        functools.partial(gather_kernel, cross),
        out_shape=(
            jax.ShapeDtypeStruct(hidden_grad.shape, jnp.bfloat16),
            jax.ShapeDtypeStruct((devices, 2, tokens.shape[0], units), jnp.bfloat16),
        ),
        in_specs=[vmem] * 3,
        out_specs=(vmem, vmem),
        scratch_shapes=[
            pltpu.VMEM((devices, 2, units, features), jnp.bfloat16),
            pltpu.VMEM((devices, 2, units, features), jnp.bfloat16),
        ]
        + [sems] * 8,
        compiler_params=pltpu.CompilerParams(
            collective_id=1, has_side_effects=True, vmem_limit_bytes=56 * 1024 * 1024
        ),
    )(tokens, hidden_grad, weights)


def scatter_kernel(
    tokens_ref, grads_ref, out_ref, near_out, near_in, ring_out, ring_in, near_send, near_recv, ring_send, ring_recv
):
    devices = lax.axis_size("blk")
    half = devices // 2
    features, units = out_ref.shape[2], out_ref.shape[1]
    blk, rep = lax.axis_index("blk"), lax.axis_index("rep")
    parity = blk % 2
    pos = (1 - parity) * (blk // 2) + parity * (devices - 1 - blk // 2)

    def at_position(q):
        late = q // half
        return (1 - late) * 2 * q + late * (2 * (devices - 1 - q) + 1)

    after = {"blk": at_position((pos + 1) % devices)}
    before = {"blk": at_position((pos + devices - 1) % devices)}
    near = {"rep": 1 - rep}
    mesh_ids = pl.DeviceIdType.MESH

    def index_of(direction, k):
        if k == half:
            return devices - 1
        return k if direction > 0 else half - 1 + k

    barrier = pltpu.get_barrier_semaphore()
    for peer in (after, before, near):
        pl.semaphore_signal(barrier, inc=1, device_id=peer, device_id_type=mesh_ids)
    pl.semaphore_wait(barrier, 3)

    started = []

    def near_copy(i, which):
        return pltpu.make_async_remote_copy(
            src_ref=near_out.at[i, which], dst_ref=near_in.at[i, which], send_sem=near_send.at[i, which],
            recv_sem=near_recv.at[i, which], device_id=near, device_id_type=mesh_ids,
        )

    def ring_copy(i, which, peer):
        return pltpu.make_async_remote_copy(
            src_ref=ring_out.at[i, which], dst_ref=ring_in.at[i, which], send_sem=ring_send.at[i, which],
            recv_sem=ring_recv.at[i, which], device_id=peer, device_id_type=mesh_ids,
        )

    own_at = pl.multiple_of(rep * features, 128)
    other_at = pl.multiple_of((1 - rep) * features, 128)
    tile = min(units, 256)
    contract = (((0,), (0,)), ((), ()))

    def product(i, which, rows, first):
        return lax.dot_general(
            grads_ref[i, which, :, rows], tokens_ref[:, pl.ds(first, features)], contract,
            preferred_element_type=jnp.float32,
        )

    def give(i, which):
        @pl.loop(0, units // tile)
        def _(t):
            rows = pl.ds(pl.multiple_of(t * tile, tile), tile)
            near_out[i, which, rows, :] = product(i, which, rows, other_at).astype(jnp.bfloat16)

        copy = near_copy(i, which)
        copy.start()
        started.append(copy)

    def keep(i, which, sources, peer):
        near_copy(i, which).wait_recv()
        for source in sources:
            ring_copy(source, which, after).wait_recv()

        @pl.loop(0, units // tile)
        def _(t):
            rows = pl.ds(pl.multiple_of(t * tile, tile), tile)
            total = product(i, which, rows, own_at) + near_in[i, which, rows, :].astype(jnp.float32)
            for source in sources:
                total = total + ring_in[source, which, rows, :].astype(jnp.float32)
            if peer is None:
                out_ref[which, rows, :] = total
            else:
                ring_out[i, which, rows, :] = total.astype(jnp.bfloat16)

        if peer is not None:
            copy = ring_copy(i, which, peer)
            copy.start()
            started.append(copy)

    def items(k):
        if k == half:
            return [(1, 0), (-1, 1)]
        if k == 0:
            return [(1, 0), (1, 1)]
        return [(1, 1), (-1, 0), (1, 0), (-1, 1)]

    for direction, which in items(half):
        give(index_of(direction, half), which)
    for k in range(half, -1, -1):
        if k > 0:
            following = items(k - 1)
        for direction, which in items(k):
            if k == half:
                sources = []
            elif k == 0:
                sources = [index_of(1, 1), index_of(-1, 1)]
            elif k == half - 1:
                sources = [devices - 1] if which == (0 if direction > 0 else 1) else []
            else:
                sources = [index_of(direction, k + 1)]
            index = index_of(direction, k) if k > 0 else 0
            keep(index, which, sources, None if k == 0 else (before if direction > 0 else after))
            if k == half:
                continue
            if k > 0 and following:
                ahead, part = following.pop(0)
                give(index_of(ahead, k - 1) if k > 1 else 0, part)
        if k == half:
            for ahead, part in items(k - 1):
                give(index_of(ahead, k - 1), part)
    for copy in started:
        copy.wait_send()


def reduced_gradient(tokens, slot_grads, features):
    devices, _, _, units = slot_grads.shape
    vmem = pl.BlockSpec(memory_space=pltpu.VMEM)
    sems = pltpu.SemaphoreType.DMA((devices, 2))
    return pl.pallas_call(
        scatter_kernel,
        out_shape=jax.ShapeDtypeStruct((2, units, features), jnp.float32),
        in_specs=[vmem] * 2,
        out_specs=vmem,
        scratch_shapes=[pltpu.VMEM((devices, 2, units, features), jnp.bfloat16)] * 4 + [sems] * 4,
        compiler_params=pltpu.CompilerParams(
            collective_id=2, has_side_effects=True, vmem_limit_bytes=56 * 1024 * 1024
        ),
    )(tokens, slot_grads)


def on_ring(tokens, hidden_grad, weights, first_moment, second_moment):
    def partner(value):
        return lax.ppermute(value, "rep", [(0, 1), (1, 0)])

    hidden, slot_grads = gathered_forward(tokens, hidden_grad, weights)

    gradient = reduced_gradient(tokens, slot_grads, weights.shape[2])
    norm_sq = summed(jnp.sum(gradient * gradient))
    own = (gradient, first_moment, second_moment, weights)
    update = adam_all(norm_sq, own, tuple(partner(value) for value in own))
    return (hidden, update)


def solution(mesh):
    placed = (
        P(("groups", "blk", "rep"), None),
        P(("groups", "blk", "rep"), None),
        P(None, "blk", "rep"),
        P(None, ("groups", "blk"), "rep"),
        P(None, ("groups", "blk"), "rep"),
    )
    devices = mesh.shape["blk"]

    def program(tokens, hidden_grad, weights, first_moment, second_moment):
        slots = hidden_grad.shape[1] * devices // weights.shape[1]
        whole_cycle = slots == devices and devices % 2 == 0 and devices >= 4 and mesh.shape["rep"] == 2 and mesh.shape["groups"] == 2
        step = jax.shard_map(
            on_ring if whole_cycle else on_device,
            mesh=mesh,
            in_specs=placed,
            out_specs=(P(("groups", "blk", "rep"), None), P(None, ("groups", "blk"), None)),
            check_vma=False,
        )
        return step(tokens, hidden_grad, weights, first_moment, second_moment)

    return program
```

```python
import functools

import jax
import jax.numpy as jnp
from jax import lax
from jax.experimental import pallas as pl
from jax.experimental.pallas import tpu as pltpu
from jax.sharding import PartitionSpec as P

clip_norm = 1.0
beta_one = 0.9
beta_two = 0.95
step_count = 10.0
adam_eps = 1e-08
decay_rate = 0.1


def shifted(value, axis, by):
    devices = lax.axis_size(axis)
    return lax.ppermute(value, axis, [(i, (i + by) % devices) for i in range(devices)])


def swiglu_terms(tokens, incoming_grad, gate_rows, up_rows):
    contract = (((1,), (1,)), ((), ()))
    gate = lax.dot_general(tokens, gate_rows, contract, preferred_element_type=jnp.float32)
    upper = lax.dot_general(tokens, up_rows, contract, preferred_element_type=jnp.float32)
    sigma = jax.nn.sigmoid(gate)
    activated = gate * sigma
    hidden = (activated * upper).astype(jnp.bfloat16)
    incoming = incoming_grad.astype(jnp.float32)
    gate_grad = (incoming * upper * sigma * (1.0 + gate * (1.0 - sigma))).astype(jnp.bfloat16)
    up_grad = (incoming * activated).astype(jnp.bfloat16)
    return (hidden, gate_grad, up_grad)


def adam_update(gradient, first_moment, second_moment, weights, norm_sq):
    clip_scale = jnp.minimum(1.0, clip_norm / jnp.sqrt(norm_sq))
    clipped = gradient * clip_scale
    first = beta_one * first_moment + (1.0 - beta_one) * clipped
    second = beta_two * second_moment + (1.0 - beta_two) * clipped * clipped
    first_hat = first / (1.0 - beta_one**step_count)
    second_hat = second / (1.0 - beta_two**step_count)
    return first_hat / (jnp.sqrt(second_hat) + adam_eps) + decay_rate * weights.astype(jnp.float32)


def on_device(tokens, hidden_grad, weights, first_moment, second_moment):
    unit_count = weights.shape[1]
    token_count = tokens.shape[0]
    slot_count = hidden_grad.shape[1] // unit_count
    own_full = lax.all_gather(weights, "rep", axis=2, tiled=True)
    slot_grads = jnp.swapaxes(hidden_grad.reshape(token_count, slot_count, unit_count), 0, 1)
    contract = (((1,), (0,)), ((), ()))

    def grad_term(gate_grad, up_grad):
        paired = jnp.stack([gate_grad, up_grad], axis=0)
        return lax.dot_general(paired, tokens, contract, preferred_element_type=jnp.float32)

    zero_sums = jnp.zeros((2, unit_count, tokens.shape[1]), jnp.float32)

    def visit(panel_rows, slot_grad):
        hidden, gate_grad, up_grad = swiglu_terms(tokens, slot_grad, panel_rows[0], panel_rows[1])
        arrived = shifted(panel_rows, "blk", 1)
        return (arrived, (hidden, gate_grad, up_grad))

    _, (hidden_slots, gate_slots, up_slots) = lax.scan(visit, own_full, slot_grads)

    def collect(running, grads_pair):
        arrived = shifted(running, "blk", -1)
        return (arrived + grad_term(grads_pair[0], grads_pair[1]), None)

    owned_sums, _ = lax.scan(collect, zero_sums, (gate_slots, up_slots), reverse=True)
    hidden = jnp.swapaxes(hidden_slots, 0, 1).reshape(token_count, slot_count * unit_count)
    gradient = lax.psum_scatter(owned_sums, "rep", scatter_dimension=2, tiled=True)
    norm_sq = lax.psum(jnp.sum(gradient * gradient), ("blk", "rep"))
    update = adam_update(gradient, first_moment, second_moment, weights, norm_sq)
    adam_step = lax.all_gather(update, "rep", axis=2, tiled=True)
    return (hidden, adam_step)


def adam_kernel(norm_ref, *refs):
    own, other, out_ref = refs[:4], refs[4:8], refs[8]
    features = own[0].shape[-1]
    scale = jnp.minimum(1.0, clip_norm / jnp.sqrt(norm_ref[0:1, 0:1]))

    def write(values, first):
        gradient, first_moment, second_moment, weights = (ref[0] for ref in values)
        clipped = gradient * scale
        moment = beta_one * first_moment + (1.0 - beta_one) * clipped
        square = beta_two * second_moment + (1.0 - beta_two) * clipped * clipped
        moment = moment * (1.0 / (1.0 - beta_one**step_count))
        square = square * (1.0 / (1.0 - beta_two**step_count))
        update = moment / (jnp.sqrt(square) + adam_eps) + decay_rate * weights.astype(jnp.float32)
        out_ref[0, :, first : first + features] = update

    rep = lax.axis_index("rep")

    @pl.when(rep == 0)
    def _():
        write(own, 0)
        write(other, features)

    @pl.when(rep != 0)
    def _():
        write(other, 0)
        write(own, features)


def adam_all(norm_sq, own, other):
    pair, units, features = own[0].shape
    tile = min(units, 128)
    block = pl.BlockSpec((1, tile, features), lambda i, j: (i, j, 0))
    return pl.pallas_call(
        adam_kernel,
        grid=(pair, units // tile),
        out_shape=jax.ShapeDtypeStruct((pair, units, 2 * features), jnp.float32),
        in_specs=[pl.BlockSpec((8, 128), lambda i, j: (0, 0))] + [block] * 8,
        out_specs=pl.BlockSpec((1, tile, 2 * features), lambda i, j: (i, j, 0)),
        compiler_params=pltpu.CompilerParams(vmem_limit_bytes=24 * 1024 * 1024),
    )(norm_sq, *own, *other)


def gather_kernel(
    cross, tokens_ref, grad_ref, weights_ref, hidden_ref, out_grads_ref, mine, other, ring_send, ring_recv,
    cross_send, cross_recv, near_send, near_recv, far_send, far_recv
):
    devices = lax.axis_size("blk")
    half = devices // 2
    units, features = weights_ref.shape[1], weights_ref.shape[2]
    token_count = tokens_ref.shape[0]
    blk, rep, group = lax.axis_index("blk"), lax.axis_index("rep"), lax.axis_index("groups")
    parity = blk % 2
    pos = (1 - parity) * (blk // 2) + parity * (devices - 1 - blk // 2)

    def at_position(q):
        late = q // half
        return (1 - late) * 2 * q + late * (2 * (devices - 1 - q) + 1)

    after = {"blk": at_position((pos + 1) % devices)}
    before = {"blk": at_position((pos + devices - 1) % devices)}
    near = {"rep": 1 - rep}
    across = {"groups": 1 - group}
    mesh_ids = pl.DeviceIdType.MESH

    ring_rows = units - cross
    ring_at = pl.multiple_of((1 - group) * cross, 16)
    give_at = pl.multiple_of((1 - group) * ring_rows, 16)
    take_at = pl.multiple_of(group * ring_rows, 16)
    whole, ring_part = pl.ds(0, units), pl.ds(ring_at, ring_rows)
    give_part, take_part = pl.ds(give_at, cross), pl.ds(take_at, cross)

    def index_of(direction, k):
        if k == half:
            return devices - 1
        return k if direction > 0 else half - 1 + k

    barrier = pltpu.get_barrier_semaphore()
    for peer in (after, before, near, across):
        pl.semaphore_signal(barrier, inc=1, device_id=peer, device_id_type=mesh_ids)
    pl.semaphore_wait(barrier, 4)

    started = []

    def send(source, target, part, send_sem, recv_sem, peer):
        copy = pltpu.make_async_remote_copy(
            src_ref=source.at[part], dst_ref=target.at[part], send_sem=send_sem, recv_sem=recv_sem,
            device_id=peer, device_id_type=mesh_ids,
        )
        copy.start()
        started.append(copy)

    def arrive(target, part, send_sem, recv_sem, peer):
        pltpu.make_async_remote_copy(
            src_ref=target.at[part], dst_ref=target.at[part], send_sem=send_sem, recv_sem=recv_sem,
            device_id=peer, device_id_type=mesh_ids,
        ).wait_recv()

    def forward(direction, k, which):
        if k + 1 == half and which != (0 if direction > 0 else 1):
            return
        source = weights_ref.at[which] if k == 0 else mine.at[index_of(direction, k), which]
        to = index_of(direction, k + 1)
        send(
            source, mine.at[to, which], ring_part, ring_send.at[to, which], ring_recv.at[to, which],
            after if direction > 0 else before,
        )

    def ring_step(direction, k, which):
        i = index_of(direction, k)
        arrive(mine.at[i, which], ring_part, ring_send.at[i, which], ring_recv.at[i, which], after)
        if k < half:
            forward(direction, k, which)
        send(mine.at[i, which], mine.at[i, which], give_part, cross_send.at[i, which], cross_recv.at[i, which], across)
        send(mine.at[i, which], other.at[i, which], ring_part, near_send.at[i, which], near_recv.at[i, which], near)

    def complete(i):
        for which in range(2):
            arrive(mine.at[i, which], take_part, cross_send.at[i, which], cross_recv.at[i, which], across)
            send(mine.at[i, which], other.at[i, which], take_part, far_send.at[i, which], far_recv.at[i, which], near)
        for which in range(2):
            arrive(other.at[i, which], ring_part, near_send.at[i, which], near_recv.at[i, which], near)
            arrive(other.at[i, which], take_part, far_send.at[i, which], far_recv.at[i, which], near)

    own_at = pl.multiple_of(rep * features, 128)
    other_at = pl.multiple_of((1 - rep) * features, 128)
    tile = min(token_count, 256)
    contract = (((1,), (1,)), ((), ()))

    def compute(i, signed):
        owner = at_position((pos - signed + devices) % devices)
        slot = (blk - owner + devices) % devices
        columns = pl.ds(pl.multiple_of(slot * units, 128), units)

        @pl.loop(0, token_count // tile)
        def _(t):
            rows = pl.ds(pl.multiple_of(t * tile, tile), tile)
            own_tokens = tokens_ref[rows, pl.ds(own_at, features)]
            other_tokens = tokens_ref[rows, pl.ds(other_at, features)]

            def product(which):
                own = weights_ref[which] if i == 0 else mine[i, which]
                return lax.dot_general(own_tokens, own, contract, preferred_element_type=jnp.float32) + lax.dot_general(
                    other_tokens, other[i, which], contract, preferred_element_type=jnp.float32
                )

            gate, upper = product(0), product(1)
            incoming = grad_ref[rows, columns].astype(jnp.float32)
            sigma = jax.nn.sigmoid(gate)
            activated = gate * sigma
            hidden_ref[rows, columns] = (activated * upper).astype(jnp.bfloat16)
            out_grads_ref[i, 0, rows, :] = (incoming * upper * sigma * (1.0 + gate * (1.0 - sigma))).astype(jnp.bfloat16)
            out_grads_ref[i, 1, rows, :] = (incoming * activated).astype(jnp.bfloat16)

    for which in range(2):
        for direction in (1, -1):
            forward(direction, 0, which)
    for which in range(2):
        send(weights_ref.at[which], other.at[0, which], whole, near_send.at[0, which], near_recv.at[0, which], near)
    for which in range(2):
        arrive(other.at[0, which], whole, near_send.at[0, which], near_recv.at[0, which], near)
    compute(0, 0)
    for k in range(1, half):
        for which, side in ((0, 1), (1, -1)):
            for direction in (1, -1):
                ring_step(direction, k, which)
            if k > 1:
                complete(index_of(side, k - 1))
                compute(index_of(side, k - 1), side * (k - 1))
    for which, side in ((0, 1), (1, -1)):
        ring_step(side, half, which)
        complete(index_of(side, half - 1))
        compute(index_of(side, half - 1), side * (half - 1))
    complete(devices - 1)
    compute(devices - 1, half)
    for copy in started:
        copy.wait_send()


def gathered_forward(tokens, hidden_grad, weights):
    devices = lax.axis_size("blk")
    units, features = weights.shape[1], weights.shape[2]
    cross = max(16, (units * 5 // 16) // 16 * 16)
    vmem = pl.BlockSpec(memory_space=pltpu.VMEM)
    sems = pltpu.SemaphoreType.DMA((devices, 2))
    return pl.pallas_call(
        functools.partial(gather_kernel, cross),
        out_shape=(
            jax.ShapeDtypeStruct(hidden_grad.shape, jnp.bfloat16),
            jax.ShapeDtypeStruct((devices, 2, tokens.shape[0], units), jnp.bfloat16),
        ),
        in_specs=[vmem] * 3,
        out_specs=(vmem, vmem),
        scratch_shapes=[
            pltpu.VMEM((devices, 2, units, features), jnp.bfloat16),
            pltpu.VMEM((devices, 2, units, features), jnp.bfloat16),
        ]
        + [sems] * 8,
        compiler_params=pltpu.CompilerParams(
            collective_id=1, has_side_effects=True, vmem_limit_bytes=56 * 1024 * 1024
        ),
    )(tokens, hidden_grad, weights)


def scatter_kernel(
    tokens_ref, grads_ref, out_ref, other_ref, norm_ref, near_out, near_in, ring_out, ring_in, squares, slots,
    near_send, near_recv, ring_send, ring_recv, swap_send, swap_recv, norm_send, norm_recv
):
    devices = lax.axis_size("blk")
    half = devices // 2
    features, units = out_ref.shape[2], out_ref.shape[1]
    blk, rep = lax.axis_index("blk"), lax.axis_index("rep")
    parity = blk % 2
    pos = (1 - parity) * (blk // 2) + parity * (devices - 1 - blk // 2)

    def at_position(q):
        late = q // half
        return (1 - late) * 2 * q + late * (2 * (devices - 1 - q) + 1)

    after = {"blk": at_position((pos + 1) % devices)}
    before = {"blk": at_position((pos + devices - 1) % devices)}
    near = {"rep": 1 - rep}
    mesh_ids = pl.DeviceIdType.MESH

    def index_of(direction, k):
        if k == half:
            return devices - 1
        return k if direction > 0 else half - 1 + k

    members = 2 * devices
    me = blk * 2 + rep

    def member(by):
        peer = (me + by) % members
        return {"blk": peer // 2, "rep": peer % 2}

    barrier = pltpu.get_barrier_semaphore()
    for by in range(1, members):
        pl.semaphore_signal(barrier, inc=1, device_id=member(by), device_id_type=mesh_ids)
    pl.semaphore_wait(barrier, members - 1)
    squares[...] = jnp.zeros_like(squares)

    started = []

    def near_copy(i, which):
        return pltpu.make_async_remote_copy(
            src_ref=near_out.at[i, which], dst_ref=near_in.at[i, which], send_sem=near_send.at[i, which],
            recv_sem=near_recv.at[i, which], device_id=near, device_id_type=mesh_ids,
        )

    def ring_copy(i, which, peer):
        return pltpu.make_async_remote_copy(
            src_ref=ring_out.at[i, which], dst_ref=ring_in.at[i, which], send_sem=ring_send.at[i, which],
            recv_sem=ring_recv.at[i, which], device_id=peer, device_id_type=mesh_ids,
        )

    def swap_copy(which):
        return pltpu.make_async_remote_copy(
            src_ref=out_ref.at[which], dst_ref=other_ref.at[which], send_sem=swap_send.at[which],
            recv_sem=swap_recv.at[which], device_id=near, device_id_type=mesh_ids,
        )

    own_at = pl.multiple_of(rep * features, 128)
    other_at = pl.multiple_of((1 - rep) * features, 128)
    tile = min(units, 256)
    contract = (((0,), (0,)), ((), ()))

    def product(i, which, rows, first):
        return lax.dot_general(
            grads_ref[i, which, :, rows], tokens_ref[:, pl.ds(first, features)], contract,
            preferred_element_type=jnp.float32,
        )

    def give(i, which):
        @pl.loop(0, units // tile)
        def _(t):
            rows = pl.ds(pl.multiple_of(t * tile, tile), tile)
            near_out[i, which, rows, :] = product(i, which, rows, other_at).astype(jnp.bfloat16)

        copy = near_copy(i, which)
        copy.start()
        started.append(copy)

    def keep(i, which, sources, peer):
        near_copy(i, which).wait_recv()
        for source in sources:
            ring_copy(source, which, after).wait_recv()

        @pl.loop(0, units // tile)
        def _(t):
            rows = pl.ds(pl.multiple_of(t * tile, tile), tile)
            total = product(i, which, rows, own_at) + near_in[i, which, rows, :].astype(jnp.float32)
            for source in sources:
                total = total + ring_in[source, which, rows, :].astype(jnp.float32)
            if peer is None:
                out_ref[which, rows, :] = total
                folded = jnp.sum((total * total).reshape(tile // 8, 8, features), axis=0)
                for lane in range(0, features, 128):
                    squares[...] += folded[:, lane : lane + 128]
            else:
                ring_out[i, which, rows, :] = total.astype(jnp.bfloat16)

        copy = swap_copy(which) if peer is None else ring_copy(i, which, peer)
        copy.start()
        started.append(copy)

    def items(k):
        if k == half:
            return [(1, 0), (-1, 1)]
        if k == 0:
            return [(1, 0), (1, 1)]
        return [(1, 1), (-1, 0), (1, 0), (-1, 1)]

    for direction, which in items(half):
        give(index_of(direction, half), which)
    for k in range(half, -1, -1):
        if k > 0:
            following = items(k - 1)
        for direction, which in items(k):
            if k == half:
                sources = []
            elif k == 0:
                sources = [index_of(1, 1), index_of(-1, 1)]
            elif k == half - 1:
                sources = [devices - 1] if which == (0 if direction > 0 else 1) else []
            else:
                sources = [index_of(direction, k + 1)]
            index = index_of(direction, k) if k > 0 else 0
            keep(index, which, sources, None if k == 0 else (before if direction > 0 else after))
            if k == half:
                continue
            if k > 0 and following:
                ahead, part = following.pop(0)
                give(index_of(ahead, k - 1) if k > 1 else 0, part)
        if k == half:
            for ahead, part in items(k - 1):
                give(index_of(ahead, k - 1), part)
    slots[me] = squares[...]
    copies = []
    for by in range(1, members):
        copy = pltpu.make_async_remote_copy(
            src_ref=squares, dst_ref=slots.at[me], send_sem=norm_send.at[by], recv_sem=norm_recv.at[by],
            device_id=member(by), device_id_type=mesh_ids,
        )
        copy.start()
        copies.append(copy)
    for copy in copies:
        copy.wait()
    total = slots[0]
    for i in range(1, members):
        total = total + slots[i]
    norm_ref[...] = jnp.full(norm_ref.shape, jnp.sum(total), jnp.float32)
    for copy in started:
        copy.wait_send()
    for which in range(2):
        swap_copy(which).wait_recv()


def reduced_gradient(tokens, slot_grads, features):
    devices, _, _, units = slot_grads.shape
    vmem = pl.BlockSpec(memory_space=pltpu.VMEM)
    sems = pltpu.SemaphoreType.DMA((devices, 2))
    return pl.pallas_call(
        scatter_kernel,
        out_shape=(
            jax.ShapeDtypeStruct((2, units, features), jnp.float32),
            jax.ShapeDtypeStruct((2, units, features), jnp.float32),
            jax.ShapeDtypeStruct((8, 128), jnp.float32),
        ),
        in_specs=[vmem] * 2,
        out_specs=(vmem, pl.BlockSpec(memory_space=pl.ANY), vmem),
        scratch_shapes=[pltpu.VMEM((devices, 2, units, features), jnp.bfloat16)] * 4
        + [pltpu.VMEM((8, 128), jnp.float32), pltpu.VMEM((2 * devices, 8, 128), jnp.float32)]
        + [sems] * 4
        + [pltpu.SemaphoreType.DMA((2,))] * 2
        + [pltpu.SemaphoreType.DMA((2 * devices,))] * 2,
        compiler_params=pltpu.CompilerParams(
            collective_id=2, has_side_effects=True, vmem_limit_bytes=56 * 1024 * 1024
        ),
    )(tokens, slot_grads)


def on_ring(tokens, hidden_grad, weights, first_moment, second_moment):
    def partner(value):
        return lax.ppermute(value, "rep", [(0, 1), (1, 0)])

    hidden, slot_grads = gathered_forward(tokens, hidden_grad, weights)

    gradient, other_gradient, norm_sq = reduced_gradient(tokens, slot_grads, weights.shape[2])
    own = (first_moment, second_moment, weights)
    other = tuple(partner(value) for value in own)
    update = adam_all(norm_sq, (gradient,) + own, (other_gradient,) + other)
    return (hidden, update)


def solution(mesh):
    placed = (
        P(("groups", "blk", "rep"), None),
        P(("groups", "blk", "rep"), None),
        P(None, "blk", "rep"),
        P(None, ("groups", "blk"), "rep"),
        P(None, ("groups", "blk"), "rep"),
    )
    devices = mesh.shape["blk"]

    def program(tokens, hidden_grad, weights, first_moment, second_moment):
        slots = hidden_grad.shape[1] * devices // weights.shape[1]
        whole_cycle = slots == devices and devices % 2 == 0 and devices >= 4 and mesh.shape["rep"] == 2 and mesh.shape["groups"] == 2
        step = jax.shard_map(
            on_ring if whole_cycle else on_device,
            mesh=mesh,
            in_specs=placed,
            out_specs=(P(("groups", "blk", "rep"), None), P(None, ("groups", "blk"), None)),
            check_vma=False,
        )
        return step(tokens, hidden_grad, weights, first_moment, second_moment)

    return program
```

```python
import functools

import jax
import jax.numpy as jnp
from jax import lax
from jax.experimental import pallas as pl
from jax.experimental.pallas import tpu as pltpu
from jax.sharding import PartitionSpec as P

clip_norm = 1.0
beta_one = 0.9
beta_two = 0.95
step_count = 10.0
adam_eps = 1e-08
decay_rate = 0.1


def shifted(value, axis, by):
    devices = lax.axis_size(axis)
    return lax.ppermute(value, axis, [(i, (i + by) % devices) for i in range(devices)])


def swiglu_terms(tokens, incoming_grad, gate_rows, up_rows):
    contract = (((1,), (1,)), ((), ()))
    gate = lax.dot_general(tokens, gate_rows, contract, preferred_element_type=jnp.float32)
    upper = lax.dot_general(tokens, up_rows, contract, preferred_element_type=jnp.float32)
    sigma = jax.nn.sigmoid(gate)
    activated = gate * sigma
    hidden = (activated * upper).astype(jnp.bfloat16)
    incoming = incoming_grad.astype(jnp.float32)
    gate_grad = (incoming * upper * sigma * (1.0 + gate * (1.0 - sigma))).astype(jnp.bfloat16)
    up_grad = (incoming * activated).astype(jnp.bfloat16)
    return (hidden, gate_grad, up_grad)


def adam_update(gradient, first_moment, second_moment, weights, norm_sq):
    clip_scale = jnp.minimum(1.0, clip_norm / jnp.sqrt(norm_sq))
    clipped = gradient * clip_scale
    first = beta_one * first_moment + (1.0 - beta_one) * clipped
    second = beta_two * second_moment + (1.0 - beta_two) * clipped * clipped
    first_hat = first / (1.0 - beta_one**step_count)
    second_hat = second / (1.0 - beta_two**step_count)
    return first_hat / (jnp.sqrt(second_hat) + adam_eps) + decay_rate * weights.astype(jnp.float32)


def on_device(tokens, hidden_grad, weights, first_moment, second_moment):
    unit_count = weights.shape[1]
    token_count = tokens.shape[0]
    slot_count = hidden_grad.shape[1] // unit_count
    own_full = lax.all_gather(weights, "rep", axis=2, tiled=True)
    slot_grads = jnp.swapaxes(hidden_grad.reshape(token_count, slot_count, unit_count), 0, 1)
    contract = (((1,), (0,)), ((), ()))

    def grad_term(gate_grad, up_grad):
        paired = jnp.stack([gate_grad, up_grad], axis=0)
        return lax.dot_general(paired, tokens, contract, preferred_element_type=jnp.float32)

    zero_sums = jnp.zeros((2, unit_count, tokens.shape[1]), jnp.float32)

    def visit(panel_rows, slot_grad):
        hidden, gate_grad, up_grad = swiglu_terms(tokens, slot_grad, panel_rows[0], panel_rows[1])
        arrived = shifted(panel_rows, "blk", 1)
        return (arrived, (hidden, gate_grad, up_grad))

    _, (hidden_slots, gate_slots, up_slots) = lax.scan(visit, own_full, slot_grads)

    def collect(running, grads_pair):
        arrived = shifted(running, "blk", -1)
        return (arrived + grad_term(grads_pair[0], grads_pair[1]), None)

    owned_sums, _ = lax.scan(collect, zero_sums, (gate_slots, up_slots), reverse=True)
    hidden = jnp.swapaxes(hidden_slots, 0, 1).reshape(token_count, slot_count * unit_count)
    gradient = lax.psum_scatter(owned_sums, "rep", scatter_dimension=2, tiled=True)
    norm_sq = lax.psum(jnp.sum(gradient * gradient), ("blk", "rep"))
    update = adam_update(gradient, first_moment, second_moment, weights, norm_sq)
    adam_step = lax.all_gather(update, "rep", axis=2, tiled=True)
    return (hidden, adam_step)


def adam_kernel(norm_ref, *refs):
    own, other, out_ref = refs[:4], refs[4:8], refs[8]
    features = own[0].shape[-1]
    scale = jnp.minimum(1.0, clip_norm / jnp.sqrt(norm_ref[0:1, 0:1]))

    def write(values, first):
        gradient, first_moment, second_moment, weights = (ref[0] for ref in values)
        clipped = gradient * scale
        moment = beta_one * first_moment + (1.0 - beta_one) * clipped
        square = beta_two * second_moment + (1.0 - beta_two) * clipped * clipped
        moment = moment * (1.0 / (1.0 - beta_one**step_count))
        square = square * (1.0 / (1.0 - beta_two**step_count))
        update = moment / (jnp.sqrt(square) + adam_eps) + decay_rate * weights.astype(jnp.float32)
        out_ref[0, :, first : first + features] = update

    rep = lax.axis_index("rep")

    @pl.when(rep == 0)
    def _():
        write(own, 0)
        write(other, features)

    @pl.when(rep != 0)
    def _():
        write(other, 0)
        write(own, features)


def adam_all(norm_sq, own, other):
    pair, units, features = own[0].shape
    tile = min(units, 256)
    block = pl.BlockSpec((1, tile, features), lambda i, j: (i, j, 0))
    return pl.pallas_call(
        adam_kernel,
        grid=(pair, units // tile),
        out_shape=jax.ShapeDtypeStruct((pair, units, 2 * features), jnp.float32),
        in_specs=[pl.BlockSpec((8, 128), lambda i, j: (0, 0))] + [block] * 8,
        out_specs=pl.BlockSpec((1, tile, 2 * features), lambda i, j: (i, j, 0)),
        compiler_params=pltpu.CompilerParams(vmem_limit_bytes=32 * 1024 * 1024),
    )(norm_sq, *own, *other)


def gather_kernel(
    cross, tokens_ref, grad_ref, weights_ref, hidden_ref, out_grads_ref, mine, other, ring_send, ring_recv,
    cross_send, cross_recv, near_send, near_recv, far_send, far_recv
):
    devices = lax.axis_size("blk")
    half = devices // 2
    units, features = weights_ref.shape[1], weights_ref.shape[2]
    token_count = tokens_ref.shape[0]
    blk, rep, group = lax.axis_index("blk"), lax.axis_index("rep"), lax.axis_index("groups")
    parity = blk % 2
    pos = (1 - parity) * (blk // 2) + parity * (devices - 1 - blk // 2)

    def at_position(q):
        late = q // half
        return (1 - late) * 2 * q + late * (2 * (devices - 1 - q) + 1)

    after = {"blk": at_position((pos + 1) % devices)}
    before = {"blk": at_position((pos + devices - 1) % devices)}
    near = {"rep": 1 - rep}
    across = {"groups": 1 - group}
    mesh_ids = pl.DeviceIdType.MESH

    ring_rows = units - cross
    ring_at = pl.multiple_of((1 - group) * cross, 16)
    give_at = pl.multiple_of((1 - group) * ring_rows, 16)
    take_at = pl.multiple_of(group * ring_rows, 16)
    whole, ring_part = pl.ds(0, units), pl.ds(ring_at, ring_rows)
    give_part, take_part = pl.ds(give_at, cross), pl.ds(take_at, cross)

    def index_of(direction, k):
        if k == half:
            return devices - 1
        return k if direction > 0 else half - 1 + k

    barrier = pltpu.get_barrier_semaphore()
    for peer in (after, before, near, across):
        pl.semaphore_signal(barrier, inc=1, device_id=peer, device_id_type=mesh_ids)
    pl.semaphore_wait(barrier, 4)

    started = []

    def send(source, target, part, send_sem, recv_sem, peer):
        copy = pltpu.make_async_remote_copy(
            src_ref=source.at[part], dst_ref=target.at[part], send_sem=send_sem, recv_sem=recv_sem,
            device_id=peer, device_id_type=mesh_ids,
        )
        copy.start()
        started.append(copy)

    def arrive(target, part, send_sem, recv_sem, peer):
        pltpu.make_async_remote_copy(
            src_ref=target.at[part], dst_ref=target.at[part], send_sem=send_sem, recv_sem=recv_sem,
            device_id=peer, device_id_type=mesh_ids,
        ).wait_recv()

    def forward(direction, k, which):
        if k + 1 == half and which != (0 if direction > 0 else 1):
            return
        source = weights_ref.at[which] if k == 0 else mine.at[index_of(direction, k), which]
        to = index_of(direction, k + 1)
        send(
            source, mine.at[to, which], ring_part, ring_send.at[to, which], ring_recv.at[to, which],
            after if direction > 0 else before,
        )

    def ring_step(direction, k, which):
        i = index_of(direction, k)
        arrive(mine.at[i, which], ring_part, ring_send.at[i, which], ring_recv.at[i, which], after)
        if k < half:
            forward(direction, k, which)
        send(mine.at[i, which], mine.at[i, which], give_part, cross_send.at[i, which], cross_recv.at[i, which], across)
        send(mine.at[i, which], other.at[i, which], ring_part, near_send.at[i, which], near_recv.at[i, which], near)

    def complete(i):
        for which in range(2):
            arrive(mine.at[i, which], take_part, cross_send.at[i, which], cross_recv.at[i, which], across)
            send(mine.at[i, which], other.at[i, which], take_part, far_send.at[i, which], far_recv.at[i, which], near)
        for which in range(2):
            arrive(other.at[i, which], ring_part, near_send.at[i, which], near_recv.at[i, which], near)
            arrive(other.at[i, which], take_part, far_send.at[i, which], far_recv.at[i, which], near)

    own_at = pl.multiple_of(rep * features, 128)
    other_at = pl.multiple_of((1 - rep) * features, 128)
    tile = min(token_count, 512)
    contract = (((1,), (1,)), ((), ()))

    def compute(i, signed):
        owner = at_position((pos - signed + devices) % devices)
        slot = (blk - owner + devices) % devices
        columns = pl.ds(pl.multiple_of(slot * units, 128), units)

        @pl.loop(0, token_count // tile)
        def _(t):
            rows = pl.ds(pl.multiple_of(t * tile, tile), tile)
            own_tokens = tokens_ref[rows, pl.ds(own_at, features)]
            other_tokens = tokens_ref[rows, pl.ds(other_at, features)]

            def product(which):
                own = weights_ref[which] if i == 0 else mine[i, which]
                return lax.dot_general(own_tokens, own, contract, preferred_element_type=jnp.float32) + lax.dot_general(
                    other_tokens, other[i, which], contract, preferred_element_type=jnp.float32
                )

            gate, upper = product(0), product(1)
            incoming = grad_ref[rows, columns].astype(jnp.float32)
            sigma = jax.nn.sigmoid(gate)
            activated = gate * sigma
            hidden_ref[rows, columns] = (activated * upper).astype(jnp.bfloat16)
            out_grads_ref[i, 0, rows, :] = (incoming * upper * sigma * (1.0 + gate * (1.0 - sigma))).astype(jnp.bfloat16)
            out_grads_ref[i, 1, rows, :] = (incoming * activated).astype(jnp.bfloat16)

    for which in range(2):
        for direction in (1, -1):
            forward(direction, 0, which)
    for which in range(2):
        send(weights_ref.at[which], other.at[0, which], whole, near_send.at[0, which], near_recv.at[0, which], near)
    for which in range(2):
        arrive(other.at[0, which], whole, near_send.at[0, which], near_recv.at[0, which], near)
    compute(0, 0)
    for k in range(1, half):
        for which, side in ((0, 1), (1, -1)):
            for direction in (1, -1):
                ring_step(direction, k, which)
            if k > 1:
                complete(index_of(side, k - 1))
                compute(index_of(side, k - 1), side * (k - 1))
    for which, side in ((0, 1), (1, -1)):
        ring_step(side, half, which)
        complete(index_of(side, half - 1))
        compute(index_of(side, half - 1), side * (half - 1))
    complete(devices - 1)
    compute(devices - 1, half)
    for copy in started:
        copy.wait_send()


def gathered_forward(tokens, hidden_grad, weights):
    devices = lax.axis_size("blk")
    units, features = weights.shape[1], weights.shape[2]
    cross = max(16, (units * 5 // 16) // 16 * 16)
    vmem = pl.BlockSpec(memory_space=pltpu.VMEM)
    sems = pltpu.SemaphoreType.DMA((devices, 2))
    return pl.pallas_call(
        functools.partial(gather_kernel, cross),
        out_shape=(
            jax.ShapeDtypeStruct(hidden_grad.shape, jnp.bfloat16),
            jax.ShapeDtypeStruct((devices, 2, tokens.shape[0], units), jnp.bfloat16),
        ),
        in_specs=[vmem] * 3,
        out_specs=(vmem, vmem),
        scratch_shapes=[
            pltpu.VMEM((devices, 2, units, features), jnp.bfloat16),
            pltpu.VMEM((devices, 2, units, features), jnp.bfloat16),
        ]
        + [sems] * 8,
        compiler_params=pltpu.CompilerParams(
            collective_id=1, has_side_effects=True, vmem_limit_bytes=56 * 1024 * 1024
        ),
    )(tokens, hidden_grad, weights)


def scatter_kernel(
    tokens_ref, grads_ref, out_ref, other_ref, norm_ref, near_out, near_in, ring_out, ring_in, squares, slots,
    near_send, near_recv, ring_send, ring_recv, swap_send, swap_recv, norm_send, norm_recv
):
    devices = lax.axis_size("blk")
    half = devices // 2
    features, units = out_ref.shape[2], out_ref.shape[1]
    blk, rep = lax.axis_index("blk"), lax.axis_index("rep")
    parity = blk % 2
    pos = (1 - parity) * (blk // 2) + parity * (devices - 1 - blk // 2)

    def at_position(q):
        late = q // half
        return (1 - late) * 2 * q + late * (2 * (devices - 1 - q) + 1)

    after = {"blk": at_position((pos + 1) % devices)}
    before = {"blk": at_position((pos + devices - 1) % devices)}
    near = {"rep": 1 - rep}
    mesh_ids = pl.DeviceIdType.MESH

    def index_of(direction, k):
        if k == half:
            return devices - 1
        return k if direction > 0 else half - 1 + k

    members = 2 * devices
    me = blk * 2 + rep

    def member(by):
        peer = (me + by) % members
        return {"blk": peer // 2, "rep": peer % 2}

    barrier = pltpu.get_barrier_semaphore()
    for by in range(1, members):
        pl.semaphore_signal(barrier, inc=1, device_id=member(by), device_id_type=mesh_ids)
    pl.semaphore_wait(barrier, members - 1)
    squares[...] = jnp.zeros_like(squares)

    started = []

    def near_copy(i, which):
        return pltpu.make_async_remote_copy(
            src_ref=near_out.at[i, which], dst_ref=near_in.at[i, which], send_sem=near_send.at[i, which],
            recv_sem=near_recv.at[i, which], device_id=near, device_id_type=mesh_ids,
        )

    def ring_copy(i, which, peer):
        return pltpu.make_async_remote_copy(
            src_ref=ring_out.at[i, which], dst_ref=ring_in.at[i, which], send_sem=ring_send.at[i, which],
            recv_sem=ring_recv.at[i, which], device_id=peer, device_id_type=mesh_ids,
        )

    def swap_copy(which):
        return pltpu.make_async_remote_copy(
            src_ref=out_ref.at[which], dst_ref=other_ref.at[which], send_sem=swap_send.at[which],
            recv_sem=swap_recv.at[which], device_id=near, device_id_type=mesh_ids,
        )

    own_at = pl.multiple_of(rep * features, 128)
    other_at = pl.multiple_of((1 - rep) * features, 128)
    tile = min(units, 256)
    contract = (((0,), (0,)), ((), ()))

    def product(i, which, rows, first):
        return lax.dot_general(
            grads_ref[i, which, :, rows], tokens_ref[:, pl.ds(first, features)], contract,
            preferred_element_type=jnp.float32,
        )

    def give(i, which):
        @pl.loop(0, units // tile)
        def _(t):
            rows = pl.ds(pl.multiple_of(t * tile, tile), tile)
            near_out[i, which, rows, :] = product(i, which, rows, other_at).astype(jnp.bfloat16)

        copy = near_copy(i, which)
        copy.start()
        started.append(copy)

    def keep(i, which, sources, peer):
        near_copy(i, which).wait_recv()
        for source in sources:
            ring_copy(source, which, after).wait_recv()

        @pl.loop(0, units // tile)
        def _(t):
            rows = pl.ds(pl.multiple_of(t * tile, tile), tile)
            total = product(i, which, rows, own_at) + near_in[i, which, rows, :].astype(jnp.float32)
            for source in sources:
                total = total + ring_in[source, which, rows, :].astype(jnp.float32)
            if peer is None:
                out_ref[which, rows, :] = total
                folded = jnp.sum((total * total).reshape(tile // 8, 8, features), axis=0)
                for lane in range(0, features, 128):
                    squares[...] += folded[:, lane : lane + 128]
            else:
                ring_out[i, which, rows, :] = total.astype(jnp.bfloat16)

        copy = swap_copy(which) if peer is None else ring_copy(i, which, peer)
        copy.start()
        started.append(copy)

    def items(k):
        if k == half:
            return [(1, 0), (-1, 1)]
        if k == 0:
            return [(1, 0), (1, 1)]
        return [(1, 1), (-1, 0), (1, 0), (-1, 1)]

    for direction, which in items(half):
        give(index_of(direction, half), which)
    for k in range(half, -1, -1):
        if k > 0:
            following = items(k - 1)
        for direction, which in items(k):
            if k == half:
                sources = []
            elif k == 0:
                sources = [index_of(1, 1), index_of(-1, 1)]
            elif k == half - 1:
                sources = [devices - 1] if which == (0 if direction > 0 else 1) else []
            else:
                sources = [index_of(direction, k + 1)]
            index = index_of(direction, k) if k > 0 else 0
            keep(index, which, sources, None if k == 0 else (before if direction > 0 else after))
            if k == half:
                continue
            if k > 0 and following:
                ahead, part = following.pop(0)
                give(index_of(ahead, k - 1) if k > 1 else 0, part)
        if k == half:
            for ahead, part in items(k - 1):
                give(index_of(ahead, k - 1), part)
    slots[me] = squares[...]
    copies = []
    for by in range(1, members):
        copy = pltpu.make_async_remote_copy(
            src_ref=squares, dst_ref=slots.at[me], send_sem=norm_send.at[by], recv_sem=norm_recv.at[by],
            device_id=member(by), device_id_type=mesh_ids,
        )
        copy.start()
        copies.append(copy)
    for copy in copies:
        copy.wait()
    total = slots[0]
    for i in range(1, members):
        total = total + slots[i]
    norm_ref[...] = jnp.full(norm_ref.shape, jnp.sum(total), jnp.float32)
    for copy in started:
        copy.wait_send()
    for which in range(2):
        swap_copy(which).wait_recv()


def reduced_gradient(tokens, slot_grads, features):
    devices, _, _, units = slot_grads.shape
    vmem = pl.BlockSpec(memory_space=pltpu.VMEM)
    sems = pltpu.SemaphoreType.DMA((devices, 2))
    return pl.pallas_call(
        scatter_kernel,
        out_shape=(
            jax.ShapeDtypeStruct((2, units, features), jnp.float32),
            jax.ShapeDtypeStruct((2, units, features), jnp.float32),
            jax.ShapeDtypeStruct((8, 128), jnp.float32),
        ),
        in_specs=[vmem] * 2,
        out_specs=(vmem, pl.BlockSpec(memory_space=pl.ANY), vmem),
        scratch_shapes=[pltpu.VMEM((devices, 2, units, features), jnp.bfloat16)] * 4
        + [pltpu.VMEM((8, 128), jnp.float32), pltpu.VMEM((2 * devices, 8, 128), jnp.float32)]
        + [sems] * 4
        + [pltpu.SemaphoreType.DMA((2,))] * 2
        + [pltpu.SemaphoreType.DMA((2 * devices,))] * 2,
        compiler_params=pltpu.CompilerParams(
            collective_id=2, has_side_effects=True, vmem_limit_bytes=56 * 1024 * 1024
        ),
    )(tokens, slot_grads)


def on_ring(tokens, hidden_grad, weights, first_moment, second_moment):
    def partner(value):
        return lax.ppermute(value, "rep", [(0, 1), (1, 0)])

    hidden, slot_grads = gathered_forward(tokens, hidden_grad, weights)

    gradient, other_gradient, norm_sq = reduced_gradient(tokens, slot_grads, weights.shape[2])
    own = (first_moment, second_moment, weights)
    other = tuple(partner(value) for value in own)
    update = adam_all(norm_sq, (gradient,) + own, (other_gradient,) + other)
    return (hidden, update)


def solution(mesh):
    placed = (
        P(("groups", "blk", "rep"), None),
        P(("groups", "blk", "rep"), None),
        P(None, "blk", "rep"),
        P(None, ("groups", "blk"), "rep"),
        P(None, ("groups", "blk"), "rep"),
    )
    devices = mesh.shape["blk"]

    def program(tokens, hidden_grad, weights, first_moment, second_moment):
        slots = hidden_grad.shape[1] * devices // weights.shape[1]
        whole_cycle = slots == devices and devices % 2 == 0 and devices >= 4 and mesh.shape["rep"] == 2 and mesh.shape["groups"] == 2
        step = jax.shard_map(
            on_ring if whole_cycle else on_device,
            mesh=mesh,
            in_specs=placed,
            out_specs=(P(("groups", "blk", "rep"), None), P(None, ("groups", "blk"), None)),
            check_vma=False,
        )
        return step(tokens, hidden_grad, weights, first_moment, second_moment)

    return program
```
